32 devices in a mesh: groups: 2 (over y), wide: 2 (over x), narrow: 4 (over z), sub: 2 (over core).
Axes of the slice: x: 2, y: 2, z: 4, core: 2. Of those that a mesh axis runs over, the one named last changes fastest.
Arguments:
- radiance: bfloat16 [1024, 64, 512], P(('groups', 'wide', 'narrow', 'sub')), parts along dimension 0, may hold values from -6 to 6
- band_mask: int32 [512], replicated, may hold values from 0 to 1, as said below
- row_counts: int32 [32], P(('groups', 'wide', 'narrow', 'sub')), parts along dimension 0, may hold values from 16 to 32, as said below
- noise_kernel: float32 [8, 512], replicated, may hold values from -1 to 1
- smooth_kernel: float32 [25, 512], replicated, may hold values from 0.01 to 0.1
- start_basis: float32 [512, 128], replicated, may hold values from -6 to 6
Outputs:
- components: float32 [1024, 64, 128], P(('groups', 'wide', 'narrow', 'sub')), parts along dimension 0
The draws below stay inside these ranges and needn't reach their ends.
There are 2 independent parts, one for each index of `groups`. The reference program is written for one: setup_inputs(seed, part) draws one part's arguments, and reference() takes and returns one part's arrays. A program takes and returns all parts, laid end to end along the dimension named above; an argument that names none is the same for every part. Nothing has to cross between parts.
Inputs may be any that keep to these rules, and one draw needn't show every extreme that they name: `band_mask`: exactly 425 of the 512 entries are 1, at bands drawn from the seed. `row_counts`: every draw holds a full device and one with half its rows valid.
All inputs are finite; a program needn't handle non-finite values.
Results may differ from the reference program's by a relative error of at most 0.0031.
Values may be sent and summed in bfloat16 or wider, within the bound.
No kernel may reach another device: no remote copies, remote signals or barrier semaphores. Data moves between devices by JAX's collectives and lax.ppermute only.
A program may use at most 192 MiB of HBM per device.

```python
import math
import jax
import jax.numpy as jnp
from jax import lax

B = 512
VALID = 425
K = 128
COLS = 64
ROWS_DEV = 32
SWEEPS = 2
SHARDS = 16
ROWS = 512


def draw_band_mask(key, part):
    order = jax.random.permutation(key, B)
    return (order < VALID).astype(jnp.int32)


def draw_row_counts(key, part):
    first_key, second_key = jax.random.split(key)
    counts = jax.random.randint(first_key, (SHARDS,), ROWS_DEV // 2, ROWS_DEV + 1)
    picks = jax.random.permutation(second_key, SHARDS)
    counts = counts.at[picks[0]].set(ROWS_DEV)
    counts = counts.at[picks[1]].set(ROWS_DEV // 2)
    return counts.astype(jnp.int32)


def levels(own_key, dims, shards, low, high):
    loudness = 1.0
    for dim, parts in shards:
        steps = jax.random.uniform(jax.random.fold_in(jax.random.fold_in(own_key, 6), dim), (parts,), jnp.float32, low / len(shards), high / len(shards))
        loudness = loudness * jnp.repeat(jnp.exp(steps), dims[dim] // parts).reshape((-1,) + (1,) * (len(dims) - 1 - dim))
    return loudness


def gaussian(own_key, extent, width, bound, shards=(), held_as=jnp.bfloat16):
    array = jax.random.normal(own_key, extent, jnp.float32) * width
    if len(shards) > 0:
        array = levels(own_key, extent, shards, -0.22, 0.18) * array
    return jnp.clip(array, min=-bound, max=bound).astype(held_as)


def setup_inputs(seed: int = 0, part: int = 0) -> dict:
    splits = jax.random.split(jax.random.key(seed), 7)
    own_keys = jax.random.split(jax.random.fold_in(splits[6], part), 7)
    return {
        "radiance": gaussian(own_keys[0], (ROWS, COLS, B), 1.0, 6.0, ((0, 16),)),
        "band_mask": draw_band_mask(jax.random.fold_in(splits[6], 71), part),
        "row_counts": draw_row_counts(jax.random.fold_in(jax.random.fold_in(splits[6], part), 71), part),
        "noise_kernel": gaussian(splits[3], (8, B), 0.25, 1.0, (), jnp.float32),
        "smooth_kernel": jnp.clip(jnp.exp(jax.random.uniform(splits[4], (25, B), jnp.float32, math.log(0.01), math.log(0.1))), 0.01, 0.1),
        "start_basis": gaussian(splits[5], (B, K), 1.0, 6.0, (), jnp.float32),
    }


def filters(padded, noise_kernel, smooth_kernel):
    height = padded.shape[0] - 4
    across = padded.shape[1]
    framed = jnp.pad(padded, ((0, 0), (2, 2), (0, 0)))
    running = framed[2:2 + height, 2:2 + across].astype(jnp.float32)
    tap_index = 0
    for row_off in (-1, 0, 1):
        for col_off in (-1, 0, 1):
            if row_off == 0 and col_off == 0:
                continue
            window = framed[2 + row_off:2 + row_off + height, 2 + col_off:2 + col_off + across]
            running = running - noise_kernel[tap_index] * window.astype(jnp.float32)
            tap_index += 1
    smooth = jnp.zeros((height // 2, across // 2, padded.shape[2]), jnp.float32)
    for row_off in range(5):
        for col_off in range(5):
            window = framed[row_off:row_off + height:2, col_off:col_off + across:2]
            smooth = smooth + smooth_kernel[row_off * 5 + col_off] * window.astype(jnp.float32)
    return (running.astype(jnp.bfloat16), smooth.astype(jnp.bfloat16))

def gram(values):
    flattened = values.reshape(-1, values.shape[-1])
    return lax.dot_general(flattened.astype(jnp.float32), flattened.astype(jnp.float32), (((0,), (0,)), ((), ())), preferred_element_type=jnp.float32)

def project(operator, lower_noise, band_keep, start_basis):
    basis_now = start_basis * band_keep[:, None]
    for sweep in range(SWEEPS):
        mapped = jnp.dot(operator, basis_now, precision=lax.Precision.HIGHEST)
        gram_small = jnp.dot(mapped.T, mapped, precision=lax.Precision.HIGHEST)
        factor = jnp.linalg.cholesky(gram_small)
        basis_now = jax.scipy.linalg.solve_triangular(factor, mapped.T, lower=True).T
    weights = jax.scipy.linalg.solve_triangular(lower_noise, basis_now, lower=True, trans=1)
    return weights.astype(jnp.bfloat16)

def finish_grams(noise_gram, signal_gram, pixel_total, band_keep, start_basis):
    pair_mask = band_keep[:, None] * band_keep[None, :]
    fill = jnp.diag(1.0 - band_keep)
    lower_noise = jnp.linalg.cholesky(noise_gram * pair_mask / pixel_total + fill)
    partial_solve = jax.scipy.linalg.solve_triangular(lower_noise, signal_gram * pair_mask + fill, lower=True)
    operator = jax.scipy.linalg.solve_triangular(lower_noise, partial_solve.T, lower=True)
    return project(operator, lower_noise, band_keep, start_basis)

def reference(radiance, band_mask, row_counts, noise_kernel, smooth_kernel, start_basis):
    band_keep = band_mask.astype(jnp.float32)
    position = jnp.arange(ROWS, dtype=jnp.int32)
    row_valid = (position % ROWS_DEV < row_counts[position // ROWS_DEV]).astype(jnp.float32)
    masked = radiance * (row_valid[:, None, None] * band_keep[None, None, :]).astype(jnp.bfloat16)
    framed = jnp.pad(masked, ((2, 2), (0, 0), (0, 0)))

    def accumulate(carry, block_index):
        start = (block_index * ROWS_DEV).astype(jnp.int32)
        piece = lax.dynamic_slice_in_dim(framed, start, ROWS_DEV + 4, 0)
        valid_here = lax.dynamic_slice_in_dim(row_valid, start, ROWS_DEV, 0)
        noise_field, signal = filters(piece, noise_kernel, smooth_kernel)
        noise_field = noise_field * valid_here[:, None, None].astype(jnp.bfloat16)
        return ((carry[0] + gram(noise_field), carry[1] + gram(signal)), None)
    zero_gram = jnp.zeros((B, B), jnp.float32)
    grams, unused = lax.scan(accumulate, (zero_gram, zero_gram), jnp.arange(SHARDS, dtype=jnp.int32))
    pixel_total = COLS * jnp.sum(row_counts).astype(jnp.float32)
    weights = finish_grams(grams[0], grams[1], pixel_total, band_keep, start_basis)
    blocks = masked.reshape(SHARDS, ROWS_DEV * COLS, B)
    result = lax.map(lambda block: jnp.dot(block.astype(jnp.float32), weights.astype(jnp.float32), preferred_element_type=jnp.float32), blocks)
    return result.reshape(ROWS, COLS, K)
```

```python
import jax
import jax.numpy as jnp
from jax import lax
from jax.experimental import pallas as pl
from jax.experimental.pallas import tpu as pltpu
from jax.sharding import PartitionSpec as P

SWEEPS = 2
VALID = 425
AXES = ("wide", "narrow", "sub")
LANES = 128
USED = 448
STARTS = (0, 448, 768, 960)
PACKED = 1024
PITCH = 72
HIGH = lax.Precision.HIGHEST
F32 = jnp.float32
BF16 = jnp.bfloat16


def mm(a, b, dims=((1,), (0,))):
    return lax.dot_general(a, b, (dims, ((), ())), precision=HIGH, preferred_element_type=F32)


def front_kernel(count_ref, low_ref, x_ref, high_ref, pick_ref, taps_ref, out_ref, xs, taps, nf, sg):
    height = x_ref.shape[0] // 64
    count = count_ref[0]
    pitch = xs.shape[0] // 4
    taps[...] = mm(taps_ref[...], pick_ref[...].astype(F32))
    xs[...] = jnp.zeros_like(xs)
    pick = pick_ref[...]

    def place(block, first_row, limit):
        values = jnp.dot(block, pick, preferred_element_type=F32)
        for k in range(block.shape[0] // 64):
            row = first_row + k
            piece = values[k * 64 : (k + 1) * 64]
            if limit is not None:
                piece = jnp.where(row < limit, piece, 0.0)
            start = pl.multiple_of(8 + (row + 2) * PITCH, 8)
            for tile in range(4):
                xs[pl.ds(start + tile * pitch, 64), :] = piece[:, tile * LANES : (tile + 1) * LANES]

    place(low_ref[...], -2, None)
    place(high_ref[...], height, None)

    def place_body(chunk, carry):
        place(x_ref[pl.ds(pl.multiple_of(chunk * 256, 256), 256), :], chunk * 4, count)
        return carry

    lax.fori_loop(0, height // 4, place_body, 0)

    def column(base, offset):
        return xs[pl.ds(base + offset, 32, stride=2), :]

    def noise_body(row, carry):
        valid = row < count
        for tile in range(4):
            lanes = slice(tile * LANES, (tile + 1) * LANES)
            tap = lambda k: taps[k : k + 1, lanes]
            even = odd = None
            for index, row_off in enumerate((-1, 0, 1)):
                base = tile * pitch + 8 + (row + 2 + row_off) * PITCH
                here_even = column(base, 0)
                next_even = column(base, 2)
                prev_odd = column(base, -1)
                here_odd = column(base, 1)
                if row_off == 0:
                    left, right = tap(3), tap(4)
                    part_even = here_even - left * prev_odd - right * here_odd
                    part_odd = here_odd - left * here_even - right * next_even
                else:
                    first = 0 if row_off == -1 else 5
                    left, mid, right = tap(first), tap(first + 1), tap(first + 2)
                    part_even = -(left * prev_odd + mid * here_even + right * here_odd)
                    part_odd = -(left * here_even + mid * here_odd + right * next_even)
                even = part_even if even is None else even + part_even
                odd = part_odd if odd is None else odd + part_odd
            start = pl.multiple_of(row * 64, 64)
            nf[pl.ds(start, 32), lanes] = jnp.where(valid, even, 0.0).astype(BF16)
            nf[pl.ds(start + 32, 32), lanes] = jnp.where(valid, odd, 0.0).astype(BF16)
        return carry

    lax.fori_loop(0, height, noise_body, 0)

    def signal_body(row, carry):
        for tile in range(4):
            lanes = slice(tile * LANES, (tile + 1) * LANES)
            total = jnp.zeros((32, LANES), F32)
            for i in range(5):
                base = tile * pitch + 8 + (2 * row + i) * PITCH
                for j in range(5):
                    k = 8 + 5 * i + j
                    total = total + taps[k : k + 1, lanes] * column(base, j - 2)
            sg[pl.ds(pl.multiple_of(row * 32, 32), 32), lanes] = total.astype(BF16)
        return carry

    lax.fori_loop(0, height // 2, signal_body, 0)

    for half, field in enumerate((nf, sg)):
        for panel in range(4):
            low = panel * LANES
            block = lax.dot_general(
                field[:, low:], field[:, low : low + LANES], (((0,), (0,)), ((), ())), preferred_element_type=F32
            )
            rows = USED - low
            start = half * PACKED + STARTS[panel]
            block = block[:rows]
            if half == 0 and panel == 3:
                corner = (lax.broadcasted_iota(jnp.int32, block.shape, 0) == 63) & (
                    lax.broadcasted_iota(jnp.int32, block.shape, 1) == 127
                )
                block = jnp.where(corner, count.astype(F32), block)
            out_ref[start : start + rows, :] = block


def front(count, low, x, high, pick, taps):
    height = x.shape[0] // 64
    vmem = pl.BlockSpec(memory_space=pltpu.VMEM)
    return pl.pallas_call(
        front_kernel,
        out_shape=jax.ShapeDtypeStruct((2 * PACKED, LANES), F32),
        in_specs=[pl.BlockSpec(memory_space=pltpu.SMEM)] + [vmem] * 5,
        out_specs=vmem,
        scratch_shapes=[
            pltpu.VMEM((4 * (8 + (height + 3) * PITCH + 8), LANES), F32),
            pltpu.VMEM((40, 512), F32),
            pltpu.VMEM((height * 64, 512), BF16),
            pltpu.VMEM((height * 16, 512), BF16),
        ],
        compiler_params=pltpu.CompilerParams(vmem_limit_bytes=48 << 20),
    )(count, low, x, high, pick, taps)


def scatter_sum(x, axis):
    n = lax.axis_size(axis)
    blocks = x.reshape(n, x.shape[0] // n, x.shape[1])
    me = lax.axis_index(axis)
    total = lax.dynamic_index_in_dim(blocks, me, 0, keepdims=False)
    got = []
    for d in range(1, n):
        piece = lax.dynamic_index_in_dim(blocks, (me + d) % n, 0, keepdims=False)
        got.append(lax.ppermute(piece, axis, [(i, (i + d) % n) for i in range(n)]))
    for piece in got:
        total = total + piece
    return total


def gather_rows(x, axis):
    n = lax.axis_size(axis)
    me = lax.axis_index(axis)
    got = [x] + [lax.ppermute(x, axis, [(i, (i + d) % n) for i in range(n)]) for d in range(1, n)]
    if n == 2:
        return jnp.where(me == 0, jnp.concatenate(got), jnp.concatenate(got[::-1]))
    stacked = jnp.stack(got)
    return jnp.concatenate([lax.dynamic_index_in_dim(stacked, (me - j) % n, 0, keepdims=False) for j in range(n)])


def total_sum(x):
    short = [axis for axis in ("sub", "wide", "narrow") if lax.axis_size(axis) <= 4]
    long = tuple(axis for axis in AXES if axis not in short)
    for axis in short:
        x = scatter_sum(x, axis)
    if long:
        x = lax.psum(x, long)
    for axis in reversed(short):
        x = gather_rows(x, axis)
    return x


def spread(x, row):
    return jnp.broadcast_to(x[row : row + 1, :], (8, LANES))


def inverse_factor(tiles, steps):
    lane = lax.broadcasted_iota(jnp.int32, (8, LANES), 1)
    sub = lax.broadcasted_iota(jnp.int32, (8, LANES), 0)
    tiles = list(tiles)
    for step in range(steps):
        base = step * 8
        inside = (lane >= base) & (lane < base + 8)

        def columns(x):
            return [jnp.broadcast_to(x[:, base + c : base + c + 1], (8, LANES)) for c in range(8)]

        head = tiles[step]
        cols = columns(head)
        head = jnp.where(inside, jnp.where(sub == lane - base, 1.0, 0.0), head)
        rows, inverses, tops = [], [], {}
        pivots = jnp.ones((8, LANES), F32)
        for r in range(8):
            pivot = spread(cols[r], r)
            inverse = 1.0 / pivot
            pivots = jnp.where(sub == r, pivot, pivots)
            row = spread(head, r)
            scale = jnp.where(sub > r, cols[r] * inverse, 0.0)
            rows.append(row)
            inverses.append(inverse)
            head = head - scale * row
            for c in range(r + 1, 8):
                tops[r, c] = spread(cols[c], r)
                cols[c] = cols[c] - scale * tops[r, c]
        tiles[step] = jnp.where(lane <= base + sub, head * lax.rsqrt(pivots), 0.0)
        for m in range(step + 1, len(tiles)):
            tile = tiles[m]
            cols = columns(tile)
            tile = jnp.where(inside, 0.0, tile)
            for r in range(8):
                scale = cols[r] * inverses[r]
                tile = tile - scale * rows[r]
                for c in range(r + 1, 8):
                    cols[c] = cols[c] - scale * tops[r, c]
            tiles[m] = tile
    return tiles


def finish_kernel(sums_ref, pick_ref, start_ref, out_ref, panels, signal, lower, inverse, work, factor):
    pick = pick_ref[...]
    total = 64.0 * sums_ref[PACKED - 1 : PACKED, LANES - 1 : LANES]

    for panel in range(4):
        rows = USED - panel * LANES
        block = sums_ref[STARTS[panel] : STARTS[panel] + rows, :] / total
        if panel == 3:
            r = lax.broadcasted_iota(jnp.int32, block.shape, 0)
            c = lax.broadcasted_iota(jnp.int32, block.shape, 1)
            block = jnp.where((r >= VALID - 384) | (c >= VALID - 384), jnp.where(r == c, 1.0, 0.0), block)
        panels[STARTS[panel] : STARTS[panel] + rows, :] = block

    signal[...] = jnp.zeros_like(signal)
    for panel in range(4):
        low = panel * LANES
        rows = USED - low
        start = PACKED + STARTS[panel]
        signal[low:USED, low : low + LANES] = sums_ref[start : start + rows, :]
        for other in range(panel + 1, 4):
            first = other * LANES
            count = min(LANES, USED - first)
            piece = sums_ref[start + first - low : start + first - low + count, :]
            signal[low : low + LANES, first : first + count] = piece.T
    r = lax.broadcasted_iota(jnp.int32, (64, LANES), 0)
    c = lax.broadcasted_iota(jnp.int32, (64, LANES), 1)
    signal[384:USED, 384:] = jnp.where((r == c) & (r >= VALID - 384), 1.0, signal[384:USED, 384:])

    inverse[...] = jnp.zeros_like(inverse)
    for j in range(4):
        start = STARTS[j]
        low = j * LANES
        size = min(LANES, USED - low)
        tiles = [panels[start + 8 * m : start + 8 * m + 8, :] for m in range(size // 8)]
        tiles = inverse_factor(tiles, 16 if j < 3 else (VALID - 384 + 7) // 8)
        for m, tile in enumerate(tiles):
            inverse[low + 8 * m : low + 8 * m + 8, low : low + LANES] = tile
        own = inverse[low : low + size, low : low + LANES]
        if j > 0:
            inverse[low : low + size, :low] = -mm(own[:, :size], lower[low : low + size, :low])
        rest = USED - low - LANES
        if rest <= 0:
            continue
        below = mm(panels[start + LANES : start + LANES + rest, :], own, ((1,), (1,)))
        work[:rest, :] = below
        for k in range(j + 1, 4):
            skip = (k - j - 1) * LANES
            rows = USED - k * LANES
            size_k = min(LANES, rows)
            update = mm(work[skip:rest, :], work[skip : skip + size_k, :], ((1,), (1,)))
            if size_k < LANES:
                panels[STARTS[k] : STARTS[k] + rows, :size_k] -= update
            else:
                panels[STARTS[k] : STARTS[k] + rows, :] -= update
        gain = mm(work[:rest, :], inverse[low : low + LANES, : low + LANES])
        if j > 0:
            lower[low + LANES : USED, :low] += gain[:, :low]
        lower[low + LANES : USED, low : low + LANES] = gain[:, low:]

    basis = mm(pick.astype(F32), start_ref[...], ((0,), (0,)))[:USED]
    for sweep in range(SWEEPS):
        turned = mm(inverse[...], basis, ((0,), (0,)))
        turned = mm(signal[...], turned)
        mapped = mm(inverse[:, :USED], turned)
        gram = mm(mapped, mapped, ((0,), (0,)))
        tiles = inverse_factor([gram[8 * m : 8 * m + 8, :] for m in range(16)], 16)
        for m, tile in enumerate(tiles):
            factor[8 * m : 8 * m + 8, :] = tile
        basis = mm(mapped, factor[...], ((1,), (1,)))
    weights = mm(inverse[...], basis, ((0,), (0,))).astype(BF16)
    out_ref[...] = jnp.dot(pick, weights, preferred_element_type=F32).astype(BF16)


def finish(sums, pick, start_basis):
    vmem = pl.BlockSpec(memory_space=pltpu.VMEM)
    return pl.pallas_call(
        finish_kernel,
        out_shape=jax.ShapeDtypeStruct((512, LANES), BF16),
        in_specs=[vmem] * 3,
        out_specs=vmem,
        scratch_shapes=[
            pltpu.VMEM((PACKED, LANES), F32),
            pltpu.VMEM((USED, 512), F32),
            pltpu.VMEM((USED, 512), F32),
            pltpu.VMEM((USED, 512), F32),
            pltpu.VMEM((USED, LANES), F32),
            pltpu.VMEM((LANES, LANES), F32),
        ],
        compiler_params=pltpu.CompilerParams(vmem_limit_bytes=48 << 20),
    )(sums, pick, start_basis)


def local(radiance, band_mask, row_counts, noise_kernel, smooth_kernel, start_basis):
    height, across, bands = radiance.shape
    count = row_counts[0]
    chain = 1
    for axis in AXES:
        chain *= lax.axis_size(axis)
    up = [(i, i + 1) for i in range(chain - 1)]
    down = [(i + 1, i) for i in range(chain - 1)]
    row = jnp.arange(height, dtype=jnp.int32)
    zero = jnp.zeros((), radiance.dtype)
    tail = jnp.where((row[-2:] < count)[:, None, None], radiance[-2:], zero)
    lead = jnp.where((row[:1] < count)[:, None, None], radiance[:1], zero)
    low = lax.ppermute(tail.reshape(2 * across, bands), AXES, up)
    high = lax.ppermute(lead.reshape(across, bands), AXES, down)

    order = jnp.arange(bands, dtype=jnp.int32)
    place = jnp.sum(jnp.where(order[None, :] < order[:, None], band_mask[None, :], 0), axis=1)
    pick = ((place[:, None] == order[None, :]) & (band_mask[:, None] == 1)).astype(BF16)
    taps = jnp.concatenate([noise_kernel, smooth_kernel, jnp.zeros((7, bands), F32)])

    flat = radiance.reshape(height * across, bands)
    sums = total_sum(front(row_counts, low, flat, high, pick, taps))
    weights = finish(sums, pick, start_basis)
    keep = jnp.repeat(row < count, across)
    masked = jnp.where(keep[:, None], flat, zero)
    result = jnp.dot(masked, weights, preferred_element_type=F32)
    return result.reshape(height, across, weights.shape[1])


def solution(mesh):
    split = P(("groups",) + AXES)
    return jax.shard_map(
        local,
        mesh=mesh,
        in_specs=(P(("groups",) + AXES, None, None), P(), split, P(), P(), P()),
        out_specs=P(("groups",) + AXES, None, None),
        check_vma=False,
    )
```

```python
import jax
import jax.numpy as jnp
from jax import lax
from jax.experimental import pallas as pl
from jax.experimental.pallas import tpu as pltpu
from jax.sharding import PartitionSpec as P

SWEEPS = 2
VALID = 425
AXES = ("wide", "narrow", "sub")
LANES = 128
USED = 432
PACKED = 832
SQUARE, THIRD, LAST = 0, 128, 256
BELOW = (304, 608, 784)
PITCH = 72
GROUP = 8
HIGH = lax.Precision.HIGHEST
F32 = jnp.float32
BF16 = jnp.bfloat16


def mm(a, b, dims=((1,), (0,))):
    return lax.dot_general(a, b, (dims, ((), ())), precision=HIGH, preferred_element_type=F32)


def front_kernel(count_ref, low_ref, x_ref, high_ref, pick_ref, taps_ref, keep_ref, send_ref, xs, taps, nf, sg):
    height = x_ref.shape[0] // 64
    count = count_ref[0]
    pitch = xs.shape[0] // 4
    taps[...] = mm(taps_ref[...], pick_ref[...].astype(F32))
    xs[...] = jnp.zeros_like(xs)
    pick = pick_ref[...]

    def place(block, first_row, limit):
        values = jnp.dot(block, pick, preferred_element_type=F32)
        for k in range(block.shape[0] // 64):
            row = first_row + k
            piece = values[k * 64 : (k + 1) * 64]
            if limit is not None:
                piece = jnp.where(row < limit, piece, 0.0)
            start = pl.multiple_of(8 + (row + 2) * PITCH, 8)
            for tile in range(4):
                xs[pl.ds(start + tile * pitch, 64), :] = piece[:, tile * LANES : (tile + 1) * LANES]

    place(low_ref[...], -2, None)
    place(high_ref[...], height, None)

    def place_body(chunk, carry):
        place(x_ref[pl.ds(pl.multiple_of(chunk * 256, 256), 256), :], chunk * 4, count)
        return carry

    lax.fori_loop(0, height // 4, place_body, 0)

    def column(base, offset):
        return xs[pl.ds(base + offset, 32, stride=2), :]

    def noise_body(row, carry):
        valid = row < count
        for tile in range(4):
            lanes = slice(tile * LANES, (tile + 1) * LANES)
            tap = lambda k: taps[k : k + 1, lanes]
            even = odd = None
            for index, row_off in enumerate((-1, 0, 1)):
                base = tile * pitch + 8 + (row + 2 + row_off) * PITCH
                here_even = column(base, 0)
                next_even = column(base, 2)
                prev_odd = column(base, -1)
                here_odd = column(base, 1)
                if row_off == 0:
                    left, right = tap(3), tap(4)
                    part_even = here_even - left * prev_odd - right * here_odd
                    part_odd = here_odd - left * here_even - right * next_even
                else:
                    first = 0 if row_off == -1 else 5
                    left, mid, right = tap(first), tap(first + 1), tap(first + 2)
                    part_even = -(left * prev_odd + mid * here_even + right * here_odd)
                    part_odd = -(left * here_even + mid * here_odd + right * next_even)
                even = part_even if even is None else even + part_even
                odd = part_odd if odd is None else odd + part_odd
            start = pl.multiple_of(row * 64, 64)
            nf[pl.ds(start, 32), lanes] = jnp.where(valid, even, 0.0).astype(BF16)
            nf[pl.ds(start + 32, 32), lanes] = jnp.where(valid, odd, 0.0).astype(BF16)
        return carry

    lax.fori_loop(0, height, noise_body, 0)

    def signal_body(row, carry):
        for tile in range(4):
            lanes = slice(tile * LANES, (tile + 1) * LANES)
            total = jnp.zeros((32, LANES), F32)
            for i in range(5):
                base = tile * pitch + 8 + (2 * row + i) * PITCH
                for j in range(5):
                    k = 8 + 5 * i + j
                    total = total + taps[k : k + 1, lanes] * column(base, j - 2)
            sg[pl.ds(pl.multiple_of(row * 32, 32), 32), lanes] = total.astype(BF16)
        return carry

    lax.fori_loop(0, height // 2, signal_body, 0)

    r = lax.broadcasted_iota(jnp.int32, (LANES, LANES), 0)
    c = lax.broadcasted_iota(jnp.int32, (LANES, LANES), 1)
    for half, field in enumerate((nf, sg)):

        def put(start, block):
            @pl.when(count_ref[1] == half)
            def _():
                keep_ref[start : start + block.shape[0], :] = block

            @pl.when(count_ref[1] != half)
            def _():
                send_ref[start : start + block.shape[0], :] = block

        corners = []
        for panel in range(4):
            low = panel * LANES
            block = lax.dot_general(
                field[:, low:], field[:, low : low + LANES], (((0,), (0,)), ((), ())), preferred_element_type=F32
            )
            corners.append(block[:LANES])
            if panel < 3:
                put(BELOW[panel], block[LANES : USED - low])
        put(SQUARE, jnp.where(r >= c, corners[0], corners[1]))
        put(THIRD, corners[2])
        diagonal = jnp.sum(jnp.where(r == c, corners[1], 0.0), axis=0, keepdims=True)
        tail = corners[3][: USED - 384]
        row = lax.broadcasted_iota(jnp.int32, tail.shape, 0)
        tail = jnp.where(row == 47, diagonal, jnp.where(row == 46, count.astype(F32), tail))
        put(LAST, tail)


def front(count, low, x, high, pick, taps):
    height = x.shape[0] // 64
    vmem = pl.BlockSpec(memory_space=pltpu.VMEM)
    return pl.pallas_call(
        front_kernel,
        out_shape=(jax.ShapeDtypeStruct((PACKED, LANES), F32),) * 2,
        in_specs=[pl.BlockSpec(memory_space=pltpu.SMEM)] + [vmem] * 5,
        out_specs=(vmem, vmem),
        scratch_shapes=[
            pltpu.VMEM((4 * (8 + (height + 3) * PITCH + 8), LANES), F32),
            pltpu.VMEM((40, 512), F32),
            pltpu.VMEM((height * 64, 512), BF16),
            pltpu.VMEM((height * 16, 512), BF16),
        ],
        compiler_params=pltpu.CompilerParams(vmem_limit_bytes=48 << 20),
    )(count, low, x, high, pick, taps)


def scatter_sum(x, axis):
    n = lax.axis_size(axis)
    blocks = x.reshape(n, x.shape[0] // n, x.shape[1])
    me = lax.axis_index(axis)
    total = lax.dynamic_index_in_dim(blocks, me, 0, keepdims=False)
    got = []
    for d in range(1, n):
        piece = lax.dynamic_index_in_dim(blocks, (me + d) % n, 0, keepdims=False)
        got.append(lax.ppermute(piece, axis, [(i, (i + d) % n) for i in range(n)]))
    for piece in got:
        total = total + piece
    return total


def gather_rows(x, axis):
    n = lax.axis_size(axis)
    me = lax.axis_index(axis)
    got = [x] + [lax.ppermute(x, axis, [(i, (i + d) % n) for i in range(n)]) for d in range(1, n)]
    if n == 2:
        return jnp.where(me == 0, jnp.concatenate(got), jnp.concatenate(got[::-1]))
    stacked = jnp.stack(got)
    return jnp.concatenate([lax.dynamic_index_in_dim(stacked, (me - j) % n, 0, keepdims=False) for j in range(n)])


def exchange(x):
    return lax.ppermute(x, "sub", [(0, 1), (1, 0)])


def total_sum(keep, send):
    x = keep + exchange(send)
    short = [axis for axis in ("wide", "narrow") if lax.axis_size(axis) <= 4]
    long = tuple(axis for axis in ("wide", "narrow") if axis not in short)
    for axis in short:
        x = scatter_sum(x, axis)
    if long:
        x = lax.psum(x, long)
    for axis in reversed(short):
        x = gather_rows(x, axis)
    return x, exchange(x)


def spread(x, row):
    return jnp.broadcast_to(x[row : row + 1, :], (8, LANES))


def three_parts(x):
    high = x.astype(BF16).astype(F32)
    rest = x - high
    mid = rest.astype(BF16).astype(F32)
    return high, mid, rest - mid


def inverse_factor(tiles):
    lane = lax.broadcasted_iota(jnp.int32, (8, LANES), 1)
    sub = lax.broadcasted_iota(jnp.int32, (8, LANES), 0)
    tiles = list(tiles)
    count = len(tiles)
    for first in range(0, count, GROUP):
        last = min(first + GROUP, count)
        ahead = None
        done = []
        for step in range(first, last):
            base = step * 8
            inside = (lane >= base) & (lane < base + 8)

            def columns(x, start):
                return [jnp.broadcast_to(x[:, start + c : start + c + 1], (8, LANES)) for c in range(8)]

            head = tiles[step]
            cols = columns(head, base) if ahead is None else ahead
            head = jnp.where(inside, jnp.where(sub == lane - base, 1.0, 0.0), head)
            pivots = jnp.ones((8, LANES), F32)
            pairs = []
            for r in (0, 2, 4, 6):
                q = r + 1
                a, b, c = spread(cols[r], r), spread(cols[q], r), spread(cols[q], q)
                det = a * c - b * b
                inv = 1.0 / det
                ai, bi, ci = a * inv, b * inv, c * inv
                u, v = cols[r], cols[q]
                below = sub > q
                alpha = jnp.where(below, u * ci - v * bi, 0.0)
                beta = jnp.where(below, v * ai - u * bi, 0.0)
                row_r, row_q = spread(head, r), spread(head, q)
                tops = {}
                for k in range(q + 1, 8):
                    tops[k] = (spread(cols[k], r), spread(cols[k], q))
                    cols[k] = cols[k] - alpha * tops[k][0] - beta * tops[k][1]
                ainv = 1.0 / a
                head = head - (alpha + jnp.where(sub == q, b * ainv, 0.0)) * row_r - beta * row_q
                pivots = jnp.where(sub == r, a, jnp.where(sub == q, det * ainv, pivots))
                pairs.append((r, ai, bi, ci, row_r, row_q, tops))
            scaled = head * lax.rsqrt(pivots)
            own = lane <= base + sub
            tiles[step] = jnp.where(own, scaled, 0.0)
            done.append((scaled, jnp.where(own | (lane >= last * 8), scaled, 0.0)))
            ahead = None
            for m in range(step + 1, last):
                tile = tiles[m]
                cols = columns(tile, base)
                if m == step + 1:
                    ahead = columns(tile, base + 8)
                tile = jnp.where(inside, 0.0, tile)
                for r, ai, bi, ci, row_r, row_q, tops in pairs:
                    u, v = cols[r], cols[r + 1]
                    alpha = u * ci - v * bi
                    beta = v * ai - u * bi
                    tile = tile - alpha * row_r - beta * row_q
                    for k in tops:
                        cols[k] = cols[k] - alpha * tops[k][0] - beta * tops[k][1]
                    if m == step + 1:
                        for c in range(8):
                            ahead[c] = ahead[c] - alpha * spread(u, c) - beta * spread(v, c)
                tiles[m] = tile
        if last < count:
            far = lane >= 8 * last
            keep = far | (lane < 8 * first)
            left = three_parts(jnp.concatenate([jnp.where(far, x, 0.0) for x, _ in done], axis=0))
            right = three_parts(jnp.concatenate([y for _, y in done], axis=0))
            left = jnp.concatenate([left[k] for k in (0, 0, 1, 0, 1, 2)], axis=0).astype(BF16)
            right = jnp.concatenate([right[k] for k in (0, 1, 0, 2, 1, 0)], axis=0).astype(BF16)
            update = lax.dot_general(left, right, (((0,), (0,)), ((), ())), preferred_element_type=F32)
            for m in range(last, count):
                tiles[m] = jnp.where(keep, tiles[m], 0.0) - update[8 * m : 8 * m + 8]
    return tiles


def factor_block(block):
    tiles = [block[8 * m : 8 * m + 8, :] for m in range(block.shape[0] // 8)]
    return jnp.concatenate(inverse_factor(tiles), axis=0)


def widen(x, width):
    return jnp.concatenate([x, jnp.zeros((x.shape[0], width - x.shape[1]), x.dtype)], axis=1)


def unpack(sums, start):
    r = lax.broadcasted_iota(jnp.int32, (LANES, LANES), 0)
    c = lax.broadcasted_iota(jnp.int32, (LANES, LANES), 1)
    part = lambda first, rows: sums[pl.ds(start + first, rows), :]
    square = part(SQUARE, LANES)
    turned = square.T
    corner = jnp.where(r >= c, square, turned)
    second = jnp.where(r == c, part(LAST + 47, 1), jnp.where(r < c, square, turned))
    blocks = [
        (corner, part(BELOW[0], USED - 128)),
        (second, part(BELOW[1], USED - 256)),
        (part(THIRD, LANES), part(BELOW[2], USED - 384)),
    ]
    return [jnp.concatenate(pair, axis=0) for pair in blocks] + [part(LAST, USED - 384)]


def fill_unit(block):
    r = lax.broadcasted_iota(jnp.int32, block.shape, 0)
    c = lax.broadcasted_iota(jnp.int32, block.shape, 1)
    return jnp.where((r >= VALID - 384) | (c >= VALID - 384), jnp.where(r == c, 1.0, 0.0), block)


def finish_kernel(side_ref, mine_ref, other_ref, pick_ref, start_ref, out_ref, sums, signal, inverse):
    side = side_ref[0]
    sums[pl.ds(pl.multiple_of(side * PACKED, 8), PACKED), :] = mine_ref[...]
    sums[pl.ds(pl.multiple_of((1 - side) * PACKED, 8), PACKED), :] = other_ref[...]

    signal[...] = jnp.zeros_like(signal)
    panels = unpack(sums, PACKED)
    panels[3] = fill_unit(panels[3])
    for panel in range(4):
        low = panel * LANES
        signal[low:USED, low : low + LANES] = panels[panel]
        for other in range(panel + 1, 4):
            first = other * LANES
            size = min(LANES, USED - first)
            signal[low : low + LANES, first : first + size] = panels[panel][first - low : first - low + size].T
    basis = mm(start_ref[...], pick_ref[...].astype(F32), ((0,), (0,)))[:, :USED]

    total = 64.0 * sums[LAST + 46 : LAST + 47, :]
    panels = [block / total for block in unpack(sums, 0)]
    panels[3] = fill_unit(panels[3])
    inverse[...] = jnp.zeros_like(inverse)
    known = None
    for j in range(4):
        low = j * LANES
        size = min(LANES, USED - low)
        own = factor_block(panels[j][:size])
        inverse[low : low + size, low : low + LANES] = own
        if j == 3:
            inverse[low:USED, :low] = -mm(own[:, :size], known)
            break
        below = mm(panels[j][LANES:], own, ((1,), (1,)))
        for k in range(j + 1, 4):
            skip = (k - j - 1) * LANES
            width = min(LANES, USED - k * LANES)
            update = mm(below[skip:], below[skip : skip + width], ((1,), (1,)))
            panels[k] = panels[k] - (update if width == LANES else widen(update, LANES))
        gain = mm(below, own)
        if j == 0:
            known = gain
        else:
            left = -mm(own, known[:LANES])
            inverse[low : low + LANES, :low] = left
            known = jnp.concatenate([known[LANES:] + mm(below, left), gain], axis=1)

    turned = mm(basis, inverse[...])
    mapped = mm(mm(turned[:, :USED], signal[...]), inverse[...], ((1,), (1,)))
    for sweep in range(SWEEPS):
        square = mm(mapped, mapped, ((1,), (1,)))
        turned = mm(mapped, inverse[...])
        if sweep + 1 < SWEEPS:
            ahead = mm(mm(turned[:, :USED], signal[...]), inverse[...], ((1,), (1,)))
        scale = factor_block(square)
        if sweep + 1 < SWEEPS:
            mapped = mm(scale, ahead)
    weights = mm(scale, turned).astype(BF16)
    out_ref[...] = lax.dot_general(
        pick_ref[...], weights, (((1,), (1,)), ((), ())), preferred_element_type=F32
    ).astype(BF16)


def finish(side, mine, other, pick, start_basis):
    vmem = pl.BlockSpec(memory_space=pltpu.VMEM)
    return pl.pallas_call(
        finish_kernel,
        out_shape=jax.ShapeDtypeStruct((512, LANES), BF16),
        in_specs=[pl.BlockSpec(memory_space=pltpu.SMEM)] + [vmem] * 4,
        out_specs=vmem,
        scratch_shapes=[
            pltpu.VMEM((2 * PACKED, LANES), F32),
            pltpu.VMEM((USED, 512), F32),
            pltpu.VMEM((USED, 512), F32),
        ],
        compiler_params=pltpu.CompilerParams(vmem_limit_bytes=48 << 20),
    )(side, mine, other, pick, start_basis)


def local(radiance, band_mask, row_counts, noise_kernel, smooth_kernel, start_basis):
    height, across, bands = radiance.shape
    count = row_counts[0]
    chain = 1
    for axis in AXES:
        chain *= lax.axis_size(axis)
    up = [(i, i + 1) for i in range(chain - 1)]
    down = [(i + 1, i) for i in range(chain - 1)]
    row = jnp.arange(height, dtype=jnp.int32)
    zero = jnp.zeros((), radiance.dtype)
    tail = jnp.where((row[-2:] < count)[:, None, None], radiance[-2:], zero)
    lead = jnp.where((row[:1] < count)[:, None, None], radiance[:1], zero)
    low = lax.ppermute(tail.reshape(2 * across, bands), AXES, up)
    high = lax.ppermute(lead.reshape(across, bands), AXES, down)

    order = jnp.arange(bands, dtype=jnp.int32)
    place = jnp.sum(jnp.where(order[None, :] < order[:, None], band_mask[None, :], 0), axis=1)
    pick = ((place[:, None] == order[None, :]) & (band_mask[:, None] == 1)).astype(BF16)
    taps = jnp.concatenate([noise_kernel, smooth_kernel, jnp.zeros((7, bands), F32)])

    flat = radiance.reshape(height * across, bands)
    side = lax.axis_index("sub").astype(jnp.int32)
    keep, send = front(jnp.stack([count, side]), low, flat, high, pick, taps)
    mine, other = total_sum(keep, send)
    weights = finish(side[None], mine, other, pick, start_basis)
    keep = jnp.repeat(row < count, across)
    masked = jnp.where(keep[:, None], flat, zero)
    result = jnp.dot(masked, weights, preferred_element_type=F32)
    return result.reshape(height, across, weights.shape[1])


def solution(mesh):
    split = P(("groups",) + AXES)
    return jax.shard_map(
        local,
        mesh=mesh,
        in_specs=(P(("groups",) + AXES, None, None), P(), split, P(), P(), P()),
        out_specs=P(("groups",) + AXES, None, None),
        check_vma=False,
    )
```

```python
import jax
import jax.numpy as jnp
from jax import lax
from jax.experimental import pallas as pl
from jax.experimental.pallas import tpu as pltpu
from jax.sharding import PartitionSpec as P

SWEEPS = 2
VALID = 425
AXES = ("wide", "narrow", "sub")
LANES = 128
USED = 432
PACKED = 832
SQUARE, THIRD, LAST = 0, 128, 256
BELOW = (304, 608, 784)
PITCH = 72
GROUP = 8
HIGH = lax.Precision.HIGHEST
F32 = jnp.float32
BF16 = jnp.bfloat16


def mm(a, b, dims=((1,), (0,))):
    return lax.dot_general(a, b, (dims, ((), ())), precision=HIGH, preferred_element_type=F32)


def place(xs, values, rows, slot, row, limit):
    pitch = xs.shape[0] // 4
    for k in range(rows):
        piece = values[k * 64 : (k + 1) * 64]
        if limit is not None:
            piece = jnp.where(row + k < limit, piece, 0.0)
        start = pl.multiple_of(8 + (slot + k) * PITCH, 8)
        for tile in range(4):
            xs[pl.ds(start + tile * pitch, 64), :] = piece[:, tile * LANES : (tile + 1) * LANES]


def clear_gaps(xs, slots):
    pitch = xs.shape[0] // 4
    zeros = jnp.zeros((8, LANES), F32)
    for tile in range(4):
        for slot in range(slots + 1):
            start = tile * pitch + slot * PITCH
            xs[start : start + 8, :] = zeros


def noise_tile(xs, taps, slot, valid, tile):
    pitch = xs.shape[0] // 4
    lanes = slice(tile * LANES, (tile + 1) * LANES)
    tap = lambda k: taps[k : k + 1, lanes]
    even = odd = None
    for row_off in (-1, 0, 1):
        base = tile * pitch + 8 + (slot + row_off) * PITCH
        here_even = xs[pl.ds(base, 32, stride=2), :]
        next_even = xs[pl.ds(base + 2, 32, stride=2), :]
        prev_odd = xs[pl.ds(base - 1, 32, stride=2), :]
        here_odd = xs[pl.ds(base + 1, 32, stride=2), :]
        if row_off == 0:
            left, right = tap(3), tap(4)
            part_even = here_even - left * prev_odd - right * here_odd
            part_odd = here_odd - left * here_even - right * next_even
        else:
            first = 0 if row_off == -1 else 5
            left, mid, right = tap(first), tap(first + 1), tap(first + 2)
            part_even = -(left * prev_odd + mid * here_even + right * here_odd)
            part_odd = -(left * here_even + mid * here_odd + right * next_even)
        even = part_even if even is None else even + part_even
        odd = part_odd if odd is None else odd + part_odd
    return jnp.where(valid, even, 0.0).astype(BF16), jnp.where(valid, odd, 0.0).astype(BF16)


def signal_tile(xs, taps, slot, tile):
    pitch = xs.shape[0] // 4
    lanes = slice(tile * LANES, (tile + 1) * LANES)
    total = None
    for i in range(5):
        base = tile * pitch + 8 + (slot + i) * PITCH
        for j in range(5):
            k = 8 + 5 * i + j
            term = taps[k : k + 1, lanes] * xs[pl.ds(base + j - 2, 32, stride=2), :]
            total = term if total is None else total + term
    return total.astype(BF16)


def packed_gram(field):
    r = lax.broadcasted_iota(jnp.int32, (LANES, LANES), 0)
    c = lax.broadcasted_iota(jnp.int32, (LANES, LANES), 1)
    corners, blocks = [], []
    for panel in range(4):
        low = panel * LANES
        block = lax.dot_general(
            field[:, low:], field[:, low : low + LANES], (((0,), (0,)), ((), ())), preferred_element_type=F32
        )
        corners.append(block[:LANES])
        if panel < 3:
            blocks.append((BELOW[panel], block[LANES : USED - low]))
    blocks.append((SQUARE, jnp.where(r >= c, corners[0], corners[1])))
    blocks.append((THIRD, corners[2]))
    diagonal = jnp.sum(jnp.where(r == c, corners[1], 0.0), axis=0, keepdims=True)
    tail = corners[3][: USED - 384]
    row = lax.broadcasted_iota(jnp.int32, tail.shape, 0)
    blocks.append((LAST, jnp.where(row == 47, diagonal, tail)))
    return blocks


def inner_kernel(
    count_ref, mask_hbm, noise_hbm, smooth_hbm, x_hbm, noise_out, signal_out, pick_ref, taps,
    x, xs, nf, sg, mask_ref, noise_ref, smooth_ref, sems, small_sems,
):
    height = x.shape[0] // 64
    bands = x.shape[1]
    chunks = sems.shape[0]
    size = x.shape[0] // chunks
    copies = [
        pltpu.make_async_copy(x_hbm.at[pl.ds(k * size, size)], x.at[pl.ds(k * size, size)], sems.at[k])
        for k in range(chunks)
    ]
    small = [
        pltpu.make_async_copy(source, target, small_sems.at[k])
        for k, (source, target) in enumerate(
            ((mask_hbm, mask_ref), (noise_hbm, noise_ref), (smooth_hbm, smooth_ref))
        )
    ]
    for copy in small + copies:
        copy.start()
    clear_gaps(xs, height)
    for copy in small:
        copy.wait()
    count = count_ref[0]
    mask = jnp.broadcast_to(mask_ref[...].astype(F32), (16, bands)).astype(BF16)
    r = lax.broadcasted_iota(jnp.int32, (bands, bands), 0)
    c = lax.broadcasted_iota(jnp.int32, (bands, bands), 1)
    ranks = jnp.where(c < r, 1.0, jnp.where(c == r, 1024.0, 0.0)).astype(BF16)
    position = lax.dot_general(ranks, mask, (((1,), (1,)), ((), ())), preferred_element_type=F32)[:, :1]
    pick_ref[...] = jnp.where(position == (c + 1024).astype(F32), 1.0, 0.0).astype(BF16)
    pick = pick_ref[...]
    wide_pick = pick.astype(F32)
    taps[:8, :] = mm(noise_ref[...], wide_pick)
    taps[8:, :] = mm(jnp.concatenate([smooth_ref[...], jnp.zeros((7, bands), F32)], axis=0), wide_pick)
    for k, copy in enumerate(copies):
        copy.wait()
        values = jnp.dot(x[k * size : (k + 1) * size, :], pick, preferred_element_type=F32)
        place(xs, values, size // 64, k * (size // 64), k * (size // 64), count)

    def noise_body(row, carry):
        start = pl.multiple_of((row - 1) * 64, 64)
        for tile in range(4):
            lanes = slice(tile * LANES, (tile + 1) * LANES)
            even, odd = noise_tile(xs, taps, row, row < count, tile)
            nf[pl.ds(start, 32), lanes] = even
            nf[pl.ds(start + 32, 32), lanes] = odd
        return carry

    lax.fori_loop(1, height - 1, noise_body, 0)

    def signal_body(row, carry):
        start = pl.multiple_of((row - 1) * 32, 32)
        for tile in range(4):
            sg[pl.ds(start, 32), tile * LANES : (tile + 1) * LANES] = signal_tile(xs, taps, 2 * row - 2, tile)
        return carry

    lax.fori_loop(1, height // 2 - 1, signal_body, 0)
    for field, out_ref in ((nf, noise_out), (sg, signal_out)):
        for start, block in packed_gram(field):
            out_ref[start : start + block.shape[0], :] = block


def edge_kernel(
    count_ref, low_hbm, x_hbm, high_hbm, pick_ref, taps, noise_ref, signal_ref, keep_ref, send_ref,
    rows, both, xs, nf, sg, sems,
):
    count, side = count_ref[0], count_ref[1]
    size = x_hbm.shape[0]
    height = size // 64
    pieces = ((low_hbm, 0, 128), (x_hbm.at[pl.ds(0, 192)], 128, 192), (x_hbm.at[pl.ds(size - 256, 256)], 320, 256), (high_hbm, 576, 64))
    copies = [
        pltpu.make_async_copy(source, rows.at[pl.ds(start, length)], sems.at[k])
        for k, (source, start, length) in enumerate(pieces)
    ]
    for copy in copies:
        copy.start()
    pick = pick_ref[...]
    clear_gaps(xs, 10)
    for copy in copies:
        copy.wait()
    values = jnp.dot(rows[...], pick, preferred_element_type=F32)
    place(xs, values[:128], 2, 0, 0, None)
    place(xs, values[128:320], 3, 2, 0, count)
    place(xs, values[320:576], 4, 5, height - 4, count)
    place(xs, values[576:], 1, 9, 0, None)
    for k, (slot, valid) in enumerate(((2, count > 0), (8, count > height - 1))):
        for tile in range(4):
            lanes = slice(tile * LANES, (tile + 1) * LANES)
            even, odd = noise_tile(xs, taps, slot, valid, tile)
            nf[k * 64 : k * 64 + 32, lanes] = even
            nf[k * 64 + 32 : k * 64 + 64, lanes] = odd
            sg[k * 32 : k * 32 + 32, lanes] = signal_tile(xs, taps, 5 * k, tile)
    for half, (field, inner) in enumerate(((nf, noise_ref), (sg, signal_ref))):
        for start, block in packed_gram(field):
            rows = block.shape[0]
            block = block + inner[start : start + rows, :]
            if start == LAST:
                row = lax.broadcasted_iota(jnp.int32, block.shape, 0)
                block = jnp.where(row == 46, count.astype(F32), block)
            both[half * PACKED + start : half * PACKED + start + rows, :] = block
    keep_ref[...] = both[pl.ds(pl.multiple_of(side * PACKED, 8), PACKED), :]
    send_ref[...] = both[pl.ds(pl.multiple_of((1 - side) * PACKED, 8), PACKED), :]


VMEM = pl.BlockSpec(memory_space=pltpu.VMEM)
SMEM = pl.BlockSpec(memory_space=pltpu.SMEM)
HBM = pl.BlockSpec(memory_space=pltpu.HBM)
PARAMS = pltpu.CompilerParams(vmem_limit_bytes=48 << 20)


def inner(count, mask, noise_kernel, smooth_kernel, x):
    height, bands = x.shape[0] // 64, x.shape[1]
    gram = jax.ShapeDtypeStruct((PACKED, LANES), F32)
    return pl.pallas_call(
        inner_kernel,
        out_shape=(gram, gram, jax.ShapeDtypeStruct((bands, bands), BF16), jax.ShapeDtypeStruct((40, bands), F32)),
        in_specs=[SMEM] + [HBM] * 4,
        out_specs=(VMEM,) * 4,
        scratch_shapes=[
            pltpu.VMEM(x.shape, BF16),
            pltpu.VMEM((4 * (16 + height * PITCH), LANES), F32),
            pltpu.VMEM(((height - 2) * 64, bands), BF16),
            pltpu.VMEM(((height // 2 - 2) * 32, bands), BF16),
            pltpu.VMEM(mask.shape, jnp.int32),
            pltpu.VMEM(noise_kernel.shape, F32),
            pltpu.VMEM(smooth_kernel.shape, F32),
            pltpu.SemaphoreType.DMA((8,)),
            pltpu.SemaphoreType.DMA((3,)),
        ],
        compiler_params=PARAMS,
        cost_estimate=pl.CostEstimate(flops=6 << 30, transcendentals=0, bytes_accessed=8 << 20),
        name="inner",
    )(count, *(pltpu.with_memory_space_constraint(a, pltpu.HBM) for a in (mask, noise_kernel, smooth_kernel, x)))


def edge(counts, low, x, high, pick, taps, noise, signal):
    bands = x.shape[1]
    gram = jax.ShapeDtypeStruct((PACKED, LANES), F32)
    return pl.pallas_call(
        edge_kernel,
        out_shape=(gram, gram),
        in_specs=[SMEM, HBM, HBM, HBM, VMEM, VMEM, VMEM, VMEM],
        out_specs=(VMEM, VMEM),
        scratch_shapes=[
            pltpu.VMEM((640, bands), BF16),
            pltpu.VMEM((2 * PACKED, LANES), F32),
            pltpu.VMEM((4 * (16 + 10 * PITCH), LANES), F32),
            pltpu.VMEM((128, bands), BF16),
            pltpu.VMEM((64, bands), BF16),
            pltpu.SemaphoreType.DMA((4,)),
        ],
        compiler_params=PARAMS,
        name="edge",
    )(counts, *(pltpu.with_memory_space_constraint(a, pltpu.HBM) for a in (low, x, high)), pick, taps, noise, signal)


def scatter_sum(parts, axis):
    n = lax.axis_size(axis)
    me = lax.axis_index(axis)

    def block(k):
        return [lax.dynamic_index_in_dim(x.reshape(n, -1, LANES), k, 0, keepdims=False) for x in parts]

    got = []
    for d in range(1, n):
        got.append(lax.ppermute(sum(block((me + d) % n)), axis, [(i, (i + d) % n) for i in range(n)]))
    return block(me) + got


def gather_rows(x, axis):
    n = lax.axis_size(axis)
    me = lax.axis_index(axis)
    got = [x] + [lax.ppermute(x, axis, [(i, (i + d) % n) for i in range(n)]) for d in range(1, n)]
    if n == 2:
        return jnp.where(me == 0, jnp.concatenate(got), jnp.concatenate(got[::-1]))
    stacked = jnp.stack(got)
    return jnp.concatenate([lax.dynamic_index_in_dim(stacked, (me - j) % n, 0, keepdims=False) for j in range(n)])


def exchange(x):
    return lax.ppermute(x, "sub", [(0, 1), (1, 0)])


def total_sum(keep, send):
    parts = [keep, exchange(send)]
    short = [axis for axis in ("wide", "narrow") if lax.axis_size(axis) <= 4]
    long = tuple(axis for axis in ("wide", "narrow") if axis not in short)
    for axis in short:
        parts = scatter_sum(parts, axis)
    x = sum(parts)
    if long:
        x = lax.psum(x, long)
    for axis in reversed(short):
        x = gather_rows(x, axis)
    return x, exchange(x)


def spread(x, row):
    return jnp.broadcast_to(x[row : row + 1, :], (8, LANES))


def three_parts(x):
    high = x.astype(BF16).astype(F32)
    rest = x - high
    mid = rest.astype(BF16).astype(F32)
    return high, mid, rest - mid


def inverse_factor(tiles):
    lane = lax.broadcasted_iota(jnp.int32, (8, LANES), 1)
    sub = lax.broadcasted_iota(jnp.int32, (8, LANES), 0)
    tiles = list(tiles)
    count = len(tiles)
    for first in range(0, count, GROUP):
        last = min(first + GROUP, count)
        ahead = None
        done = []
        for step in range(first, last):
            base = step * 8
            inside = (lane >= base) & (lane < base + 8)

            def columns(x, start):
                return [jnp.broadcast_to(x[:, start + c : start + c + 1], (8, LANES)) for c in range(8)]

            head = tiles[step]
            cols = columns(head, base) if ahead is None else ahead
            head = jnp.where(inside, jnp.where(sub == lane - base, 1.0, 0.0), head)
            pivots = jnp.ones((8, LANES), F32)
            pairs = []
            for r in (0, 2, 4, 6):
                q = r + 1
                a, b, c = spread(cols[r], r), spread(cols[q], r), spread(cols[q], q)
                det = a * c - b * b
                inv = 1.0 / det
                ai, bi, ci = a * inv, b * inv, c * inv
                u, v = cols[r], cols[q]
                below = sub > q
                alpha = jnp.where(below, u * ci - v * bi, 0.0)
                beta = jnp.where(below, v * ai - u * bi, 0.0)
                row_r, row_q = spread(head, r), spread(head, q)
                tops = {}
                for k in range(q + 1, 8):
                    tops[k] = (spread(cols[k], r), spread(cols[k], q))
                    cols[k] = cols[k] - alpha * tops[k][0] - beta * tops[k][1]
                ainv = 1.0 / a
                head = head - (alpha + jnp.where(sub == q, b * ainv, 0.0)) * row_r - beta * row_q
                pivots = jnp.where(sub == r, a, jnp.where(sub == q, det * ainv, pivots))
                pairs.append((r, ai, bi, ci, row_r, row_q, tops))
            scaled = head * lax.rsqrt(pivots)
            own = lane <= base + sub
            tiles[step] = jnp.where(own, scaled, 0.0)
            done.append((scaled, jnp.where(own | (lane >= last * 8), scaled, 0.0)))
            ahead = None
            for m in range(step + 1, last):
                tile = tiles[m]
                cols = columns(tile, base)
                if m == step + 1:
                    ahead = columns(tile, base + 8)
                tile = jnp.where(inside, 0.0, tile)
                for r, ai, bi, ci, row_r, row_q, tops in pairs:
                    u, v = cols[r], cols[r + 1]
                    alpha = u * ci - v * bi
                    beta = v * ai - u * bi
                    tile = tile - alpha * row_r - beta * row_q
                    for k in tops:
                        cols[k] = cols[k] - alpha * tops[k][0] - beta * tops[k][1]
                    if m == step + 1:
                        for c in range(8):
                            ahead[c] = ahead[c] - alpha * spread(u, c) - beta * spread(v, c)
                tiles[m] = tile
        if last < count:
            far = lane >= 8 * last
            keep = far | (lane < 8 * first)
            left = three_parts(jnp.concatenate([jnp.where(far, x, 0.0) for x, _ in done], axis=0))
            right = three_parts(jnp.concatenate([y for _, y in done], axis=0))
            left = jnp.concatenate([left[k] for k in (0, 0, 1, 0, 1, 2)], axis=0).astype(BF16)
            right = jnp.concatenate([right[k] for k in (0, 1, 0, 2, 1, 0)], axis=0).astype(BF16)
            update = lax.dot_general(left, right, (((0,), (0,)), ((), ())), preferred_element_type=F32)
            for m in range(last, count):
                tiles[m] = jnp.where(keep, tiles[m], 0.0) - update[8 * m : 8 * m + 8]
    return tiles


def factor_block(block):
    tiles = [block[8 * m : 8 * m + 8, :] for m in range(block.shape[0] // 8)]
    return jnp.concatenate(inverse_factor(tiles), axis=0)


def widen(x, width):
    return jnp.concatenate([x, jnp.zeros((x.shape[0], width - x.shape[1]), x.dtype)], axis=1)


def unpack(sums, start):
    r = lax.broadcasted_iota(jnp.int32, (LANES, LANES), 0)
    c = lax.broadcasted_iota(jnp.int32, (LANES, LANES), 1)
    part = lambda first, rows: sums[pl.ds(start + first, rows), :]
    square = part(SQUARE, LANES)
    turned = square.T
    corner = jnp.where(r >= c, square, turned)
    second = jnp.where(r == c, part(LAST + 47, 1), jnp.where(r < c, square, turned))
    blocks = [
        (corner, part(BELOW[0], USED - 128)),
        (second, part(BELOW[1], USED - 256)),
        (part(THIRD, LANES), part(BELOW[2], USED - 384)),
    ]
    return [jnp.concatenate(pair, axis=0) for pair in blocks] + [part(LAST, USED - 384)]


def fill_unit(block):
    r = lax.broadcasted_iota(jnp.int32, block.shape, 0)
    c = lax.broadcasted_iota(jnp.int32, block.shape, 1)
    return jnp.where((r >= VALID - 384) | (c >= VALID - 384), jnp.where(r == c, 1.0, 0.0), block)


def finish_kernel(side_ref, mine_ref, other_ref, pick_ref, start_ref, out_ref, sums, signal, inverse):
    side = side_ref[0]
    sums[pl.ds(pl.multiple_of(side * PACKED, 8), PACKED), :] = mine_ref[...]
    sums[pl.ds(pl.multiple_of((1 - side) * PACKED, 8), PACKED), :] = other_ref[...]

    signal[...] = jnp.zeros_like(signal)
    panels = unpack(sums, PACKED)
    panels[3] = fill_unit(panels[3])
    for panel in range(4):
        low = panel * LANES
        signal[low:USED, low : low + LANES] = panels[panel]
        for other in range(panel + 1, 4):
            first = other * LANES
            size = min(LANES, USED - first)
            signal[low : low + LANES, first : first + size] = panels[panel][first - low : first - low + size].T
    basis = mm(start_ref[...], pick_ref[...].astype(F32), ((0,), (0,)))[:, :USED]

    total = 64.0 * sums[LAST + 46 : LAST + 47, :]
    panels = [block / total for block in unpack(sums, 0)]
    panels[3] = fill_unit(panels[3])
    inverse[...] = jnp.zeros_like(inverse)
    known = None
    for j in range(4):
        low = j * LANES
        size = min(LANES, USED - low)
        own = factor_block(panels[j][:size])
        inverse[low : low + size, low : low + LANES] = own
        if j == 3:
            inverse[low:USED, :low] = -mm(own[:, :size], known)
            break
        below = mm(panels[j][LANES:], own, ((1,), (1,)))
        for k in range(j + 1, 4):
            skip = (k - j - 1) * LANES
            width = min(LANES, USED - k * LANES)
            update = mm(below[skip:], below[skip : skip + width], ((1,), (1,)))
            panels[k] = panels[k] - (update if width == LANES else widen(update, LANES))
        gain = mm(below, own)
        if j == 0:
            known = gain
        else:
            left = -mm(own, known[:LANES])
            inverse[low : low + LANES, :low] = left
            known = jnp.concatenate([known[LANES:] + mm(below, left), gain], axis=1)

    turned = mm(basis, inverse[...])
    mapped = mm(mm(turned[:, :USED], signal[...]), inverse[...], ((1,), (1,)))
    for sweep in range(SWEEPS):
        square = mm(mapped, mapped, ((1,), (1,)))
        turned = mm(mapped, inverse[...])
        if sweep + 1 < SWEEPS:
            ahead = mm(mm(turned[:, :USED], signal[...]), inverse[...], ((1,), (1,)))
        scale = factor_block(square)
        if sweep + 1 < SWEEPS:
            mapped = mm(scale, ahead)
    weights = mm(scale, turned).astype(BF16)
    out_ref[...] = lax.dot_general(
        pick_ref[...], weights, (((1,), (1,)), ((), ())), preferred_element_type=F32
    ).astype(BF16)


def finish(side, mine, other, pick, start_basis):
    vmem = pl.BlockSpec(memory_space=pltpu.VMEM)
    return pl.pallas_call(
        finish_kernel,
        out_shape=jax.ShapeDtypeStruct((512, LANES), BF16),
        in_specs=[pl.BlockSpec(memory_space=pltpu.SMEM)] + [vmem] * 4,
        out_specs=vmem,
        scratch_shapes=[
            pltpu.VMEM((2 * PACKED, LANES), F32),
            pltpu.VMEM((USED, 512), F32),
            pltpu.VMEM((USED, 512), F32),
        ],
        compiler_params=pltpu.CompilerParams(vmem_limit_bytes=48 << 20),
    )(side, mine, other, pick, start_basis)


def local(radiance, band_mask, row_counts, noise_kernel, smooth_kernel, start_basis):
    height, across, bands = radiance.shape
    count = row_counts[0]
    chain = 1
    for axis in AXES:
        chain *= lax.axis_size(axis)
    up = [(i, i + 1) for i in range(chain - 1)]
    down = [(i + 1, i) for i in range(chain - 1)]
    row = jnp.arange(height, dtype=jnp.int32)
    zero = jnp.zeros((), radiance.dtype)
    tail = jnp.where((row[-2:] < count)[:, None, None], radiance[-2:], zero)
    lead = jnp.where((row[:1] < count)[:, None, None], radiance[:1], zero)
    low = lax.ppermute(tail.reshape(2 * across, bands), AXES, up)
    high = lax.ppermute(lead.reshape(across, bands), AXES, down)

    flat = radiance.reshape(height * across, bands)
    noise, signal, pick, taps = inner(row_counts, band_mask[None], noise_kernel, smooth_kernel, flat)
    side = lax.axis_index("sub").astype(jnp.int32)
    counts = jnp.stack([count, side])
    keep, send = edge(counts, low, flat, high, pick, taps, noise, signal)
    mine, other = total_sum(keep, send)
    weights = finish(side[None], mine, other, pick, start_basis)
    keep = jnp.repeat(row < count, across)
    masked = jnp.where(keep[:, None], flat, zero)
    result = jnp.dot(masked, weights, preferred_element_type=F32)
    return result.reshape(height, across, weights.shape[1])


def solution(mesh):
    split = P(("groups",) + AXES)
    return jax.shard_map(
        local,
        mesh=mesh,
        in_specs=(P(("groups",) + AXES, None, None), P(), split, P(), P(), P()),
        out_specs=P(("groups",) + AXES, None, None),
        check_vma=False,
    )
```

```python
import jax
import jax.numpy as jnp
from jax import lax
from jax.experimental import pallas as pl
from jax.experimental.pallas import tpu as pltpu
from jax.sharding import PartitionSpec as P

SWEEPS = 2
VALID = 425
AXES = ("wide", "narrow", "sub")
LANES = 128
USED = 432
PACKED = 832
SQUARE, THIRD, LAST = 0, 128, 256
BELOW = (304, 608, 784)
PITCH = 72
GROUP = 8
HIGH = lax.Precision.HIGHEST
F32 = jnp.float32
BF16 = jnp.bfloat16


def mm(a, b, dims=((1,), (0,))):
    return lax.dot_general(a, b, (dims, ((), ())), precision=HIGH, preferred_element_type=F32)


def place(xs, values, rows, slot, row, limit):
    pitch = xs.shape[0] // 4
    for k in range(rows):
        piece = values[k * 64 : (k + 1) * 64]
        if limit is not None:
            piece = jnp.where(row + k < limit, piece, 0.0)
        start = pl.multiple_of(8 + (slot + k) * PITCH, 8)
        for tile in range(4):
            xs[pl.ds(start + tile * pitch, 64), :] = piece[:, tile * LANES : (tile + 1) * LANES]


def clear_gaps(xs, slots):
    pitch = xs.shape[0] // 4
    zeros = jnp.zeros((8, LANES), F32)
    for tile in range(4):
        for slot in range(slots + 1):
            start = tile * pitch + slot * PITCH
            xs[start : start + 8, :] = zeros


def noise_tile(xs, taps, slot, valid, tile):
    pitch = xs.shape[0] // 4
    lanes = slice(tile * LANES, (tile + 1) * LANES)
    tap = lambda k: taps[k : k + 1, lanes]
    even = odd = None
    for row_off in (-1, 0, 1):
        base = tile * pitch + 8 + (slot + row_off) * PITCH
        here_even = xs[pl.ds(base, 32, stride=2), :]
        next_even = xs[pl.ds(base + 2, 32, stride=2), :]
        prev_odd = xs[pl.ds(base - 1, 32, stride=2), :]
        here_odd = xs[pl.ds(base + 1, 32, stride=2), :]
        if row_off == 0:
            left, right = tap(3), tap(4)
            part_even = here_even - left * prev_odd - right * here_odd
            part_odd = here_odd - left * here_even - right * next_even
        else:
            first = 0 if row_off == -1 else 5
            left, mid, right = tap(first), tap(first + 1), tap(first + 2)
            part_even = -(left * prev_odd + mid * here_even + right * here_odd)
            part_odd = -(left * here_even + mid * here_odd + right * next_even)
        even = part_even if even is None else even + part_even
        odd = part_odd if odd is None else odd + part_odd
    return jnp.where(valid, even, 0.0).astype(BF16), jnp.where(valid, odd, 0.0).astype(BF16)


def signal_tile(xs, taps, slot, tile):
    pitch = xs.shape[0] // 4
    lanes = slice(tile * LANES, (tile + 1) * LANES)
    total = None
    for i in range(5):
        base = tile * pitch + 8 + (slot + i) * PITCH
        for j in range(5):
            k = 8 + 5 * i + j
            term = taps[k : k + 1, lanes] * xs[pl.ds(base + j - 2, 32, stride=2), :]
            total = term if total is None else total + term
    return total.astype(BF16)


def panel_grams(field):
    return [
        lax.dot_general(
            field[:, low:], field[:, low : low + LANES], (((0,), (0,)), ((), ())), preferred_element_type=F32
        )
        for low in range(0, 4 * LANES, LANES)
    ]


def packed(panels):
    r = lax.broadcasted_iota(jnp.int32, (LANES, LANES), 0)
    c = lax.broadcasted_iota(jnp.int32, (LANES, LANES), 1)
    corners = [block[:LANES] for block in panels]
    blocks = [(BELOW[k], panels[k][LANES : USED - k * LANES]) for k in range(3)]
    blocks.append((SQUARE, jnp.where(r >= c, corners[0], corners[1])))
    blocks.append((THIRD, corners[2]))
    diagonal = jnp.sum(jnp.where(r == c, corners[1], 0.0), axis=0, keepdims=True)
    tail = corners[3][: USED - 384]
    row = lax.broadcasted_iota(jnp.int32, tail.shape, 0)
    blocks.append((LAST, jnp.where(row == 47, diagonal, tail)))
    return blocks


def inner_kernel(
    count_ref, mask_hbm, noise_hbm, smooth_hbm, x_hbm, noise_out, signal_out, pick_ref, taps,
    x, xs, nf, sg, sums, mask_ref, noise_ref, smooth_ref, sems, small_sems,
):
    height = x.shape[0] // 64
    bands = x.shape[1]
    chunks = sems.shape[0]
    size = x.shape[0] // chunks
    copies = [
        pltpu.make_async_copy(x_hbm.at[pl.ds(k * size, size)], x.at[pl.ds(k * size, size)], sems.at[k])
        for k in range(chunks)
    ]
    small = [
        pltpu.make_async_copy(source, target, small_sems.at[k])
        for k, (source, target) in enumerate(
            ((mask_hbm, mask_ref), (noise_hbm, noise_ref), (smooth_hbm, smooth_ref))
        )
    ]
    for copy in small + copies:
        copy.start()
    clear_gaps(xs, height)
    for copy in small:
        copy.wait()
    count = count_ref[0]
    mask = jnp.broadcast_to(mask_ref[...].astype(F32), (16, bands)).astype(BF16)
    r = lax.broadcasted_iota(jnp.int32, (bands, bands), 0)
    c = lax.broadcasted_iota(jnp.int32, (bands, bands), 1)
    ranks = jnp.where(c < r, 1.0, jnp.where(c == r, 1024.0, 0.0)).astype(BF16)
    position = lax.dot_general(ranks, mask, (((1,), (1,)), ((), ())), preferred_element_type=F32)[:, :1]
    pick_ref[...] = jnp.where(position == (c + 1024).astype(F32), 1.0, 0.0).astype(BF16)
    pick = pick_ref[...]
    weights = jnp.concatenate([noise_ref[...], smooth_ref[...], jnp.zeros((7, bands), F32)], axis=0)
    weights = jnp.concatenate(three_parts(weights), axis=0).astype(BF16)
    weights = jnp.dot(weights, pick, preferred_element_type=F32)
    taps[...] = weights[:40] + (weights[40:80] + weights[80:])
    for copy in copies:
        copy.wait()

    def picked(k):
        return jnp.dot(x[pl.ds(pl.multiple_of(k * 256, 256), 256), :], pick, preferred_element_type=F32)

    def noise_row(row):
        start = pl.multiple_of((row + 1) * 64, 64)
        for tile in range(4):
            lanes = slice(tile * LANES, (tile + 1) * LANES)
            even, odd = noise_tile(xs, taps, row, row < count, tile)
            nf[pl.ds(start, 32), lanes] = even
            nf[pl.ds(start + 32, 32), lanes] = odd

    def add_gram(k):
        chunk = nf[pl.ds(pl.multiple_of(k * 256, 256), 256), :]
        for panel in range(4):
            low = panel * LANES
            sums[panel, low:, :] += lax.dot_general(
                chunk[:, low:], chunk[:, low : low + LANES], (((0,), (0,)), ((), ())), preferred_element_type=F32
            )

    groups = height // 4
    place(xs, picked(0), 4, 0, 0, count)
    place(xs, picked(1), 4, 4, 4, count)
    sums[...] = jnp.zeros_like(sums)
    nf[:128, :] = jnp.zeros((128, bands), BF16)
    noise_row(1)
    noise_row(2)

    def body(k, carry):
        following = jnp.minimum(k + 1, groups - 1)
        values = picked(following)
        add_gram(k - 1)
        for row in range(4):
            noise_row(4 * k - 1 + row)
        for half in range(2):
            slot = 4 * k - 4 + 2 * half
            start = pl.multiple_of((2 * k - 2 + half) * 32, 32)
            for tile in range(4):
                sg[pl.ds(start, 32), tile * LANES : (tile + 1) * LANES] = signal_tile(xs, taps, slot, tile)
        place(xs, values, 4, following * 4, following * 4, count)
        return carry

    lax.fori_loop(1, groups, body, 0)
    add_gram(groups - 1)
    corners = [[sums[panel, panel * LANES :, :] for panel in range(4)], panel_grams(sg)]
    for panels, out_ref in zip(corners, (noise_out, signal_out)):
        for start, block in packed(panels):
            out_ref[start : start + block.shape[0], :] = block


def edge_kernel(
    count_ref, low_hbm, x_hbm, high_hbm, pick_ref, taps, noise_ref, signal_ref, keep_ref, send_ref,
    rows, both, xs, nf, sg, sems,
):
    count, side = count_ref[0], count_ref[1]
    size = x_hbm.shape[0]
    height = size // 64
    pieces = ((low_hbm, 0, 128), (x_hbm.at[pl.ds(0, 192)], 128, 192), (x_hbm.at[pl.ds(size - 256, 256)], 320, 256), (high_hbm, 576, 64))
    copies = [
        pltpu.make_async_copy(source, rows.at[pl.ds(start, length)], sems.at[k])
        for k, (source, start, length) in enumerate(pieces)
    ]
    for copy in copies:
        copy.start()
    pick = pick_ref[...]
    clear_gaps(xs, 10)
    for copy in copies:
        copy.wait()
    values = jnp.dot(rows[...], pick, preferred_element_type=F32)
    place(xs, values[:128], 2, 0, 0, None)
    place(xs, values[128:320], 3, 2, 0, count)
    place(xs, values[320:576], 4, 5, height - 4, count)
    place(xs, values[576:], 1, 9, 0, None)
    for k, (slot, valid) in enumerate(((2, count > 0), (8, count > height - 1))):
        for tile in range(4):
            lanes = slice(tile * LANES, (tile + 1) * LANES)
            even, odd = noise_tile(xs, taps, slot, valid, tile)
            nf[k * 64 : k * 64 + 32, lanes] = even
            nf[k * 64 + 32 : k * 64 + 64, lanes] = odd
            sg[k * 32 : k * 32 + 32, lanes] = signal_tile(xs, taps, 5 * k, tile)
    for half, (field, inner) in enumerate(((nf, noise_ref), (sg, signal_ref))):
        for start, block in packed(panel_grams(field)):
            rows = block.shape[0]
            block = block + inner[start : start + rows, :]
            if start == LAST:
                row = lax.broadcasted_iota(jnp.int32, block.shape, 0)
                block = jnp.where(row == 46, count.astype(F32), block)
            both[half * PACKED + start : half * PACKED + start + rows, :] = block
    keep_ref[...] = both[pl.ds(pl.multiple_of(side * PACKED, 8), PACKED), :]
    send_ref[...] = both[pl.ds(pl.multiple_of((1 - side) * PACKED, 8), PACKED), :]


VMEM = pl.BlockSpec(memory_space=pltpu.VMEM)
SMEM = pl.BlockSpec(memory_space=pltpu.SMEM)
HBM = pl.BlockSpec(memory_space=pltpu.HBM)
PARAMS = pltpu.CompilerParams(vmem_limit_bytes=20 << 20)


def inner(count, mask, noise_kernel, smooth_kernel, x):
    height, bands = x.shape[0] // 64, x.shape[1]
    gram = jax.ShapeDtypeStruct((PACKED, LANES), F32)
    return pl.pallas_call(
        inner_kernel,
        out_shape=(gram, gram, jax.ShapeDtypeStruct((bands, bands), BF16), jax.ShapeDtypeStruct((40, bands), F32)),
        in_specs=[SMEM] + [HBM] * 4,
        out_specs=(VMEM,) * 4,
        scratch_shapes=[
            pltpu.VMEM(x.shape, BF16),
            pltpu.VMEM((4 * (16 + height * PITCH), LANES), F32),
            pltpu.VMEM((height * 64, bands), BF16),
            pltpu.VMEM(((height // 2 - 2) * 32, bands), BF16),
            pltpu.VMEM((4, bands, LANES), F32),
            pltpu.VMEM(mask.shape, jnp.int32),
            pltpu.VMEM(noise_kernel.shape, F32),
            pltpu.VMEM(smooth_kernel.shape, F32),
            pltpu.SemaphoreType.DMA((8,)),
            pltpu.SemaphoreType.DMA((3,)),
        ],
        compiler_params=PARAMS,
        cost_estimate=pl.CostEstimate(flops=6 << 30, transcendentals=0, bytes_accessed=8 << 20),
        name="inner",
    )(count, *(pltpu.with_memory_space_constraint(a, pltpu.HBM) for a in (mask, noise_kernel, smooth_kernel, x)))


def edge(counts, low, x, high, pick, taps, noise, signal):
    bands = x.shape[1]
    gram = jax.ShapeDtypeStruct((PACKED, LANES), F32)
    return pl.pallas_call(
        edge_kernel,
        out_shape=(gram, gram),
        in_specs=[SMEM, HBM, HBM, HBM, VMEM, VMEM, VMEM, VMEM],
        out_specs=(VMEM, VMEM),
        scratch_shapes=[
            pltpu.VMEM((640, bands), BF16),
            pltpu.VMEM((2 * PACKED, LANES), F32),
            pltpu.VMEM((4 * (16 + 10 * PITCH), LANES), F32),
            pltpu.VMEM((128, bands), BF16),
            pltpu.VMEM((64, bands), BF16),
            pltpu.SemaphoreType.DMA((4,)),
        ],
        compiler_params=PARAMS,
        name="edge",
    )(counts, *(pltpu.with_memory_space_constraint(a, pltpu.HBM) for a in (low, x, high)), pick, taps, noise, signal)


def scatter_sum(parts, axis):
    n = lax.axis_size(axis)
    me = lax.axis_index(axis)

    def block(k):
        return [lax.dynamic_index_in_dim(x.reshape(n, -1, LANES), k, 0, keepdims=False) for x in parts]

    got = []
    for d in range(1, n):
        got.append(lax.ppermute(sum(block((me + d) % n)), axis, [(i, (i + d) % n) for i in range(n)]))
    return block(me) + got


def gather_rows(x, axis):
    n = lax.axis_size(axis)
    me = lax.axis_index(axis)
    got = [x] + [lax.ppermute(x, axis, [(i, (i + d) % n) for i in range(n)]) for d in range(1, n)]
    if n == 2:
        return jnp.where(me == 0, jnp.concatenate(got), jnp.concatenate(got[::-1]))
    stacked = jnp.stack(got)
    return jnp.concatenate([lax.dynamic_index_in_dim(stacked, (me - j) % n, 0, keepdims=False) for j in range(n)])


def exchange(x):
    return lax.ppermute(x, "sub", [(0, 1), (1, 0)])


def total_sum(keep, send):
    parts = [keep, exchange(send)]
    short = [axis for axis in ("wide", "narrow") if lax.axis_size(axis) <= 4]
    long = tuple(axis for axis in ("wide", "narrow") if axis not in short)
    for axis in short:
        parts = scatter_sum(parts, axis)
    x = sum(parts)
    if long:
        x = lax.psum(x, long)
    for axis in reversed(short):
        x = gather_rows(x, axis)
    return x, exchange(x)


def spread(x, row):
    return jnp.broadcast_to(x[row : row + 1, :], (8, LANES))


def three_parts(x):
    high = x.astype(BF16).astype(F32)
    rest = x - high
    mid = rest.astype(BF16).astype(F32)
    return high, mid, rest - mid


def inverse_factor(tiles):
    lane = lax.broadcasted_iota(jnp.int32, (8, LANES), 1)
    sub = lax.broadcasted_iota(jnp.int32, (8, LANES), 0)
    tiles = list(tiles)
    count = len(tiles)
    for first in range(0, count, GROUP):
        last = min(first + GROUP, count)
        ahead = None
        done = []
        for step in range(first, last):
            base = step * 8
            inside = (lane >= base) & (lane < base + 8)

            def columns(x, start):
                return [jnp.broadcast_to(x[:, start + c : start + c + 1], (8, LANES)) for c in range(8)]

            head = tiles[step]
            cols = columns(head, base) if ahead is None else ahead
            head = jnp.where(inside, jnp.where(sub == lane - base, 1.0, 0.0), head)
            pivots = jnp.ones((8, LANES), F32)
            pairs = []
            for r in (0, 2, 4, 6):
                q = r + 1
                a, b, c = spread(cols[r], r), spread(cols[q], r), spread(cols[q], q)
                det = a * c - b * b
                inv = 1.0 / det
                ai, bi, ci = a * inv, b * inv, c * inv
                u, v = cols[r], cols[q]
                below = sub > q
                alpha = jnp.where(below, u * ci - v * bi, 0.0)
                beta = jnp.where(below, v * ai - u * bi, 0.0)
                row_r, row_q = spread(head, r), spread(head, q)
                tops = {}
                for k in range(q + 1, 8):
                    tops[k] = (spread(cols[k], r), spread(cols[k], q))
                    cols[k] = cols[k] - alpha * tops[k][0] - beta * tops[k][1]
                ainv = 1.0 / a
                head = head - (alpha + jnp.where(sub == q, b * ainv, 0.0)) * row_r - beta * row_q
                pivots = jnp.where(sub == r, a, jnp.where(sub == q, det * ainv, pivots))
                pairs.append((r, ai, bi, ci, row_r, row_q, tops))
            scaled = head * lax.rsqrt(pivots)
            own = lane <= base + sub
            tiles[step] = jnp.where(own, scaled, 0.0)
            done.append((scaled, jnp.where(own | (lane >= last * 8), scaled, 0.0)))
            ahead = None
            for m in range(step + 1, last):
                tile = tiles[m]
                cols = columns(tile, base)
                if m == step + 1:
                    ahead = columns(tile, base + 8)
                tile = jnp.where(inside, 0.0, tile)
                for r, ai, bi, ci, row_r, row_q, tops in pairs:
                    u, v = cols[r], cols[r + 1]
                    alpha = u * ci - v * bi
                    beta = v * ai - u * bi
                    tile = tile - alpha * row_r - beta * row_q
                    for k in tops:
                        cols[k] = cols[k] - alpha * tops[k][0] - beta * tops[k][1]
                    if m == step + 1:
                        for c in range(8):
                            ahead[c] = ahead[c] - alpha * spread(u, c) - beta * spread(v, c)
                tiles[m] = tile
        if last < count:
            far = lane >= 8 * last
            keep = far | (lane < 8 * first)
            left = three_parts(jnp.concatenate([jnp.where(far, x, 0.0) for x, _ in done], axis=0))
            right = three_parts(jnp.concatenate([y for _, y in done], axis=0))
            left = jnp.concatenate([left[k] for k in (0, 0, 1, 0, 1, 2)], axis=0).astype(BF16)
            right = jnp.concatenate([right[k] for k in (0, 1, 0, 2, 1, 0)], axis=0).astype(BF16)
            update = lax.dot_general(left, right, (((0,), (0,)), ((), ())), preferred_element_type=F32)
            for m in range(last, count):
                tiles[m] = jnp.where(keep, tiles[m], 0.0) - update[8 * m : 8 * m + 8]
    return tiles


def factor_block(block):
    tiles = [block[8 * m : 8 * m + 8, :] for m in range(block.shape[0] // 8)]
    return jnp.concatenate(inverse_factor(tiles), axis=0)


def widen(x, width):
    return jnp.concatenate([x, jnp.zeros((x.shape[0], width - x.shape[1]), x.dtype)], axis=1)


def unpack(sums, start):
    r = lax.broadcasted_iota(jnp.int32, (LANES, LANES), 0)
    c = lax.broadcasted_iota(jnp.int32, (LANES, LANES), 1)
    part = lambda first, rows: sums[pl.ds(start + first, rows), :]
    square = part(SQUARE, LANES)
    turned = square.T
    corner = jnp.where(r >= c, square, turned)
    second = jnp.where(r == c, part(LAST + 47, 1), jnp.where(r < c, square, turned))
    blocks = [
        (corner, part(BELOW[0], USED - 128)),
        (second, part(BELOW[1], USED - 256)),
        (part(THIRD, LANES), part(BELOW[2], USED - 384)),
    ]
    return [jnp.concatenate(pair, axis=0) for pair in blocks] + [part(LAST, USED - 384)]


def fill_unit(block):
    r = lax.broadcasted_iota(jnp.int32, block.shape, 0)
    c = lax.broadcasted_iota(jnp.int32, block.shape, 1)
    return jnp.where((r >= VALID - 384) | (c >= VALID - 384), jnp.where(r == c, 1.0, 0.0), block)


def finish_kernel(side_ref, mine_ref, other_ref, pick_ref, start_ref, out_ref, sums, signal, inverse):
    side = side_ref[0]
    sums[pl.ds(pl.multiple_of(side * PACKED, 8), PACKED), :] = mine_ref[...]
    sums[pl.ds(pl.multiple_of((1 - side) * PACKED, 8), PACKED), :] = other_ref[...]

    signal[...] = jnp.zeros_like(signal)
    panels = unpack(sums, PACKED)
    panels[3] = fill_unit(panels[3])
    for panel in range(4):
        low = panel * LANES
        signal[low:USED, low : low + LANES] = panels[panel]
        for other in range(panel + 1, 4):
            first = other * LANES
            size = min(LANES, USED - first)
            signal[low : low + LANES, first : first + size] = panels[panel][first - low : first - low + size].T
    basis = mm(start_ref[...], pick_ref[...].astype(F32), ((0,), (0,)))[:, :USED]

    total = 64.0 * sums[LAST + 46 : LAST + 47, :]
    panels = [block / total for block in unpack(sums, 0)]
    panels[3] = fill_unit(panels[3])
    inverse[...] = jnp.zeros_like(inverse)
    known = None
    for j in range(4):
        low = j * LANES
        size = min(LANES, USED - low)
        own = factor_block(panels[j][:size])
        inverse[low : low + size, low : low + LANES] = own
        if j == 3:
            inverse[low:USED, :low] = -mm(own[:, :size], known)
            break
        below = mm(panels[j][LANES:], own, ((1,), (1,)))
        for k in range(j + 1, 4):
            skip = (k - j - 1) * LANES
            width = min(LANES, USED - k * LANES)
            update = mm(below[skip:], below[skip : skip + width], ((1,), (1,)))
            panels[k] = panels[k] - (update if width == LANES else widen(update, LANES))
        gain = mm(below, own)
        if j == 0:
            known = gain
        else:
            left = -mm(own, known[:LANES])
            inverse[low : low + LANES, :low] = left
            known = jnp.concatenate([known[LANES:] + mm(below, left), gain], axis=1)

    turned = mm(basis, inverse[...])
    mapped = mm(mm(turned[:, :USED], signal[...]), inverse[...], ((1,), (1,)))
    for sweep in range(SWEEPS):
        square = mm(mapped, mapped, ((1,), (1,)))
        turned = mm(mapped, inverse[...])
        if sweep + 1 < SWEEPS:
            ahead = mm(mm(turned[:, :USED], signal[...]), inverse[...], ((1,), (1,)))
        scale = factor_block(square)
        if sweep + 1 < SWEEPS:
            mapped = mm(scale, ahead)
    weights = mm(scale, turned).astype(BF16)
    out_ref[...] = lax.dot_general(
        pick_ref[...], weights, (((1,), (1,)), ((), ())), preferred_element_type=F32
    ).astype(BF16)


def finish(side, mine, other, pick, start_basis):
    vmem = pl.BlockSpec(memory_space=pltpu.VMEM)
    return pl.pallas_call(
        finish_kernel,
        out_shape=jax.ShapeDtypeStruct((512, LANES), BF16),
        in_specs=[pl.BlockSpec(memory_space=pltpu.SMEM)] + [vmem] * 4,
        out_specs=vmem,
        scratch_shapes=[
            pltpu.VMEM((2 * PACKED, LANES), F32),
            pltpu.VMEM((USED, 512), F32),
            pltpu.VMEM((USED, 512), F32),
        ],
        compiler_params=pltpu.CompilerParams(vmem_limit_bytes=20 << 20),
    )(side, mine, other, pick, start_basis)


def local(radiance, band_mask, row_counts, noise_kernel, smooth_kernel, start_basis):
    height, across, bands = radiance.shape
    count = row_counts[0]
    chain = 1
    for axis in AXES:
        chain *= lax.axis_size(axis)
    up = [(i, i + 1) for i in range(chain - 1)]
    down = [(i + 1, i) for i in range(chain - 1)]
    row = jnp.arange(height, dtype=jnp.int32)
    zero = jnp.zeros((), radiance.dtype)
    tail = jnp.where((row[-2:] < count)[:, None, None], radiance[-2:], zero)
    lead = jnp.where((row[:1] < count)[:, None, None], radiance[:1], zero)
    low = lax.ppermute(tail.reshape(2 * across, bands), AXES, up)
    high = lax.ppermute(lead.reshape(across, bands), AXES, down)

    flat = radiance.reshape(height * across, bands)
    noise, signal, pick, taps = inner(row_counts, band_mask[None], noise_kernel, smooth_kernel, flat)
    side = lax.axis_index("sub").astype(jnp.int32)
    counts = jnp.stack([count, side])
    keep, send = edge(counts, low, flat, high, pick, taps, noise, signal)
    mine, other = total_sum(keep, send)
    weights = finish(side[None], mine, other, pick, start_basis)
    keep = jnp.repeat(row < count, across)
    masked = jnp.where(keep[:, None], flat, zero)
    result = jnp.dot(masked, weights, preferred_element_type=F32)
    return result.reshape(height, across, weights.shape[1])


def solution(mesh):
    split = P(("groups",) + AXES)
    return jax.shard_map(
        local,
        mesh=mesh,
        in_specs=(P(("groups",) + AXES, None, None), P(), split, P(), P(), P()),
        out_specs=P(("groups",) + AXES, None, None),
        check_vma=False,
    )
```

```python
import jax
import jax.numpy as jnp
from jax import lax
from jax.experimental import pallas as pl
from jax.experimental.pallas import tpu as pltpu
from jax.sharding import PartitionSpec as P

SWEEPS = 2
VALID = 425
AXES = ("wide", "narrow", "sub")
LANES = 128
USED = 432
PACKED = 832
SQUARE, THIRD, LAST = 0, 128, 256
BELOW = (304, 608, 784)
PITCH = 72
GROUP = 8
HIGH = lax.Precision.HIGHEST
F32 = jnp.float32
BF16 = jnp.bfloat16


def mm(a, b, dims=((1,), (0,))):
    return lax.dot_general(a, b, (dims, ((), ())), precision=HIGH, preferred_element_type=F32)


def place(xs, values, rows, slot, row, limit):
    pitch = xs.shape[0] // 4
    for k in range(rows):
        piece = values[k * 64 : (k + 1) * 64]
        if limit is not None:
            piece = jnp.where(row + k < limit, piece, 0.0)
        start = pl.multiple_of(8 + (slot + k) * PITCH, 8)
        for tile in range(4):
            xs[pl.ds(start + tile * pitch, 64), :] = piece[:, tile * LANES : (tile + 1) * LANES]


def clear_gaps(xs, slots):
    pitch = xs.shape[0] // 4
    zeros = jnp.zeros((8, LANES), F32)
    for tile in range(4):
        for slot in range(slots + 1):
            start = tile * pitch + slot * PITCH
            xs[start : start + 8, :] = zeros


def noise_tile(xs, taps, slot, valid, tile):
    pitch = xs.shape[0] // 4
    lanes = slice(tile * LANES, (tile + 1) * LANES)
    tap = lambda k: taps[k : k + 1, lanes]
    even = odd = None
    for row_off in (-1, 0, 1):
        base = tile * pitch + 8 + (slot + row_off) * PITCH
        here_even = xs[pl.ds(base, 32, stride=2), :]
        next_even = xs[pl.ds(base + 2, 32, stride=2), :]
        prev_odd = xs[pl.ds(base - 1, 32, stride=2), :]
        here_odd = xs[pl.ds(base + 1, 32, stride=2), :]
        if row_off == 0:
            left, right = tap(3), tap(4)
            part_even = here_even - left * prev_odd - right * here_odd
            part_odd = here_odd - left * here_even - right * next_even
        else:
            first = 0 if row_off == -1 else 5
            left, mid, right = tap(first), tap(first + 1), tap(first + 2)
            part_even = -(left * prev_odd + mid * here_even + right * here_odd)
            part_odd = -(left * here_even + mid * here_odd + right * next_even)
        even = part_even if even is None else even + part_even
        odd = part_odd if odd is None else odd + part_odd
    return jnp.where(valid, even, 0.0).astype(BF16), jnp.where(valid, odd, 0.0).astype(BF16)


def signal_tile(xs, taps, slot, tile, valid=None):
    pitch = xs.shape[0] // 4
    lanes = slice(tile * LANES, (tile + 1) * LANES)
    total = None
    for i in range(5):
        base = tile * pitch + 8 + (slot + i) * PITCH
        for j in range(5):
            k = 8 + 5 * i + j
            term = taps[k : k + 1, lanes] * xs[pl.ds(base + j - 2, 32, stride=2), :]
            total = term if total is None else total + term
    if valid is not None:
        total = jnp.where(valid, total, 0.0)
    return total.astype(BF16)


def panel_grams(field):
    return [
        lax.dot_general(
            field[:, low:], field[:, low : low + LANES], (((0,), (0,)), ((), ())), preferred_element_type=F32
        )
        for low in range(0, 4 * LANES, LANES)
    ]


def packed(panels):
    r = lax.broadcasted_iota(jnp.int32, (LANES, LANES), 0)
    c = lax.broadcasted_iota(jnp.int32, (LANES, LANES), 1)
    corners = [block[:LANES] for block in panels]
    blocks = [(BELOW[k], panels[k][LANES : USED - k * LANES]) for k in range(3)]
    blocks.append((SQUARE, jnp.where(r >= c, corners[0], corners[1])))
    blocks.append((THIRD, corners[2]))
    diagonal = jnp.sum(jnp.where(r == c, corners[1], 0.0), axis=0, keepdims=True)
    tail = corners[3][: USED - 384]
    row = lax.broadcasted_iota(jnp.int32, tail.shape, 0)
    blocks.append((LAST, jnp.where(row == 47, diagonal, tail)))
    return blocks


def inner_kernel(
    count_ref, mask_hbm, noise_hbm, smooth_hbm, x_hbm, noise_out, signal_out, pick_ref, taps,
    x, xs, nf, sg, sums, mask_ref, noise_ref, smooth_ref, sems, small_sems,
):
    height = x.shape[0] // 64
    bands = x.shape[1]
    chunks = sems.shape[0]
    size = x.shape[0] // chunks
    copies = [
        pltpu.make_async_copy(x_hbm.at[pl.ds(k * size, size)], x.at[pl.ds(k * size, size)], sems.at[k])
        for k in range(chunks)
    ]
    small = [
        pltpu.make_async_copy(source, target, small_sems.at[k])
        for k, (source, target) in enumerate(
            ((mask_hbm, mask_ref), (noise_hbm, noise_ref), (smooth_hbm, smooth_ref))
        )
    ]
    for copy in small + copies:
        copy.start()
    clear_gaps(xs, height)
    for copy in small:
        copy.wait()
    count = count_ref[0]
    mask = jnp.broadcast_to(mask_ref[...].astype(F32), (16, bands)).astype(BF16)
    r = lax.broadcasted_iota(jnp.int32, (bands, bands), 0)
    c = lax.broadcasted_iota(jnp.int32, (bands, bands), 1)
    ranks = jnp.where(c < r, 1.0, jnp.where(c == r, 1024.0, 0.0)).astype(BF16)
    position = lax.dot_general(ranks, mask, (((1,), (1,)), ((), ())), preferred_element_type=F32)[:, :1]
    pick_ref[...] = jnp.where(position == (c + 1024).astype(F32), 1.0, 0.0).astype(BF16)
    pick = pick_ref[...]
    weights = jnp.concatenate([noise_ref[...], smooth_ref[...], jnp.zeros((7, bands), F32)], axis=0)
    weights = jnp.concatenate(three_parts(weights), axis=0).astype(BF16)
    weights = jnp.dot(weights, pick, preferred_element_type=F32)
    taps[...] = weights[:40] + (weights[40:80] + weights[80:])
    for copy in copies:
        copy.wait()

    def picked(k):
        return jnp.dot(x[pl.ds(pl.multiple_of(k * 256, 256), 256), :], pick, preferred_element_type=F32)

    def noise_row(row):
        start = pl.multiple_of((row + 1) * 64, 64)
        for tile in range(4):
            lanes = slice(tile * LANES, (tile + 1) * LANES)
            even, odd = noise_tile(xs, taps, row, row < count, tile)
            nf[pl.ds(start, 32), lanes] = even
            nf[pl.ds(start + 32, 32), lanes] = odd

    def add_gram(k):
        chunk = nf[pl.ds(pl.multiple_of(k * 256, 256), 256), :]
        for panel in range(4):
            low = panel * LANES
            sums[panel, low:, :] += lax.dot_general(
                chunk[:, low:], chunk[:, low : low + LANES], (((0,), (0,)), ((), ())), preferred_element_type=F32
            )

    groups = height // 4
    place(xs, picked(0), 4, 0, 0, count)
    place(xs, picked(1), 4, 4, 4, count)
    sums[...] = jnp.zeros_like(sums)
    nf[:128, :] = jnp.zeros((128, bands), BF16)
    noise_row(1)
    noise_row(2)

    def body(k, carry):
        following = jnp.minimum(k + 1, groups - 1)
        values = picked(following)
        add_gram(k - 1)
        for row in range(4):
            noise_row(4 * k - 1 + row)
        for half in range(2):
            slot = 4 * k - 4 + 2 * half
            start = pl.multiple_of((2 * k - 2 + half) * 32, 32)
            for tile in range(4):
                sg[pl.ds(start, 32), tile * LANES : (tile + 1) * LANES] = signal_tile(xs, taps, slot, tile)
        place(xs, values, 4, following * 4, following * 4, count)
        return carry

    lax.fori_loop(1, groups, body, 0)
    add_gram(groups - 1)
    corners = [[sums[panel, panel * LANES :, :] for panel in range(4)], panel_grams(sg)]
    for panels, out_ref in zip(corners, (noise_out, signal_out)):
        for start, block in packed(panels):
            out_ref[start : start + block.shape[0], :] = block


def edge_kernel(
    state_ref, low_hbm, x_hbm, pick_ref, taps, noise_ref, signal_ref, keep_ref, send_ref, rows, both, xs, nf, sg, sems
):
    count, side, first, last = [state_ref[k] for k in range(4)]
    size = x_hbm.shape[0]
    height = size // 64
    pieces = ((low_hbm, 0, 272), (x_hbm.at[pl.ds(0, 192)], 272, 192), (x_hbm.at[pl.ds(size - 256, 256)], 464, 256))
    copies = [
        pltpu.make_async_copy(source, rows.at[pl.ds(start, length)], sems.at[k])
        for k, (source, start, length) in enumerate(pieces)
    ]
    for copy in copies:
        copy.start()
    pick = pick_ref[...]
    clear_gaps(xs, 12)
    pitch = xs.shape[0] // 4
    for tile in range(4):
        start = tile * pitch + 8 + 11 * PITCH
        xs[start : start + 64, :] = jnp.zeros((64, LANES), F32)
    for copy in copies:
        copy.wait()
    values = jnp.dot(rows[...], pick, preferred_element_type=F32)
    place(xs, values[:256], 4, 0, 0, None)
    place(xs, values[272:464], 3, 4, 0, count)
    place(xs, values[464:], 4, 7, height - 4, count)
    before = jnp.broadcast_to(rows[256:272, :LANES].astype(F32)[:1], (32, LANES))
    noise_rows = ((3, before > float(height - 1)), (4, count > 0), (10, (last == 1) & (count > height - 1)))
    signal_rows = ((0, first == 0), (2, None), (7, last == 1))
    for tile in range(4):
        lanes = slice(tile * LANES, (tile + 1) * LANES)
        for k, (slot, valid) in enumerate(noise_rows):
            even, odd = noise_tile(xs, taps, slot, valid, tile)
            nf[k * 64 : k * 64 + 32, lanes] = even
            nf[k * 64 + 32 : k * 64 + 64, lanes] = odd
        for k, (slot, valid) in enumerate(signal_rows):
            sg[k * 32 : k * 32 + 32, lanes] = signal_tile(xs, taps, slot, tile, valid)
    for half, (field, inner) in enumerate(((nf, noise_ref), (sg, signal_ref))):
        for start, block in packed(panel_grams(field)):
            length = block.shape[0]
            block = block + inner[start : start + length, :]
            if start == LAST:
                row = lax.broadcasted_iota(jnp.int32, block.shape, 0)
                block = jnp.where(row == 46, count.astype(F32), block)
            both[half * PACKED + start : half * PACKED + start + length, :] = block
    keep_ref[...] = both[pl.ds(pl.multiple_of(side * PACKED, 8), PACKED), :]
    send_ref[...] = both[pl.ds(pl.multiple_of((1 - side) * PACKED, 8), PACKED), :]


VMEM = pl.BlockSpec(memory_space=pltpu.VMEM)
SMEM = pl.BlockSpec(memory_space=pltpu.SMEM)
HBM = pl.BlockSpec(memory_space=pltpu.HBM)
PARAMS = pltpu.CompilerParams(vmem_limit_bytes=20 << 20)


def inner(count, mask, noise_kernel, smooth_kernel, x):
    height, bands = x.shape[0] // 64, x.shape[1]
    gram = jax.ShapeDtypeStruct((PACKED, LANES), F32)
    return pl.pallas_call(
        inner_kernel,
        out_shape=(gram, gram, jax.ShapeDtypeStruct((bands, bands), BF16), jax.ShapeDtypeStruct((40, bands), F32)),
        in_specs=[SMEM] + [HBM] * 4,
        out_specs=(VMEM,) * 4,
        scratch_shapes=[
            pltpu.VMEM(x.shape, BF16),
            pltpu.VMEM((4 * (16 + height * PITCH), LANES), F32),
            pltpu.VMEM((height * 64, bands), BF16),
            pltpu.VMEM(((height // 2 - 2) * 32, bands), BF16),
            pltpu.VMEM((4, bands, LANES), F32),
            pltpu.VMEM(mask.shape, jnp.int32),
            pltpu.VMEM(noise_kernel.shape, F32),
            pltpu.VMEM(smooth_kernel.shape, F32),
            pltpu.SemaphoreType.DMA((8,)),
            pltpu.SemaphoreType.DMA((3,)),
        ],
        compiler_params=PARAMS,
        cost_estimate=pl.CostEstimate(flops=6 << 30, transcendentals=0, bytes_accessed=8 << 20),
        name="inner",
    )(count, *(pltpu.with_memory_space_constraint(a, pltpu.HBM) for a in (mask, noise_kernel, smooth_kernel, x)))


def edge(state, low, x, pick, taps, noise, signal):
    bands = x.shape[1]
    gram = jax.ShapeDtypeStruct((PACKED, LANES), F32)
    return pl.pallas_call(
        edge_kernel,
        out_shape=(gram, gram),
        in_specs=[SMEM, HBM, HBM, VMEM, VMEM, VMEM, VMEM],
        out_specs=(VMEM, VMEM),
        scratch_shapes=[
            pltpu.VMEM((720, bands), BF16),
            pltpu.VMEM((2 * PACKED, LANES), F32),
            pltpu.VMEM((4 * (16 + 12 * PITCH), LANES), F32),
            pltpu.VMEM((192, bands), BF16),
            pltpu.VMEM((96, bands), BF16),
            pltpu.SemaphoreType.DMA((3,)),
        ],
        compiler_params=PARAMS,
        name="edge",
    )(state, *(pltpu.with_memory_space_constraint(a, pltpu.HBM) for a in (low, x)), pick, taps, noise, signal)


def scatter_sum(parts, axis):
    n = lax.axis_size(axis)
    me = lax.axis_index(axis)

    def block(k):
        return [lax.dynamic_index_in_dim(x.reshape(n, -1, LANES), k, 0, keepdims=False) for x in parts]

    got = []
    for d in range(1, n):
        got.append(lax.ppermute(sum(block((me + d) % n)), axis, [(i, (i + d) % n) for i in range(n)]))
    return block(me) + got


def gather_rows(x, axis):
    n = lax.axis_size(axis)
    me = lax.axis_index(axis)
    got = [x] + [lax.ppermute(x, axis, [(i, (i + d) % n) for i in range(n)]) for d in range(1, n)]
    if n == 2:
        return jnp.where(me == 0, jnp.concatenate(got), jnp.concatenate(got[::-1]))
    stacked = jnp.stack(got)
    return jnp.concatenate([lax.dynamic_index_in_dim(stacked, (me - j) % n, 0, keepdims=False) for j in range(n)])


def exchange(x):
    return lax.ppermute(x, "sub", [(0, 1), (1, 0)])


def total_sum(keep, send):
    parts = [keep, exchange(send)]
    short = [axis for axis in ("wide", "narrow") if lax.axis_size(axis) <= 4]
    long = tuple(axis for axis in ("wide", "narrow") if axis not in short)
    for axis in short:
        parts = scatter_sum(parts, axis)
    x = sum(parts)
    if long:
        x = lax.psum(x, long)
    for axis in reversed(short):
        x = gather_rows(x, axis)
    return x, exchange(x)


def spread(x, row):
    return jnp.broadcast_to(x[row : row + 1, :], (8, LANES))


def three_parts(x):
    high = x.astype(BF16).astype(F32)
    rest = x - high
    mid = rest.astype(BF16).astype(F32)
    return high, mid, rest - mid


def inverse_factor(tiles):
    lane = lax.broadcasted_iota(jnp.int32, (8, LANES), 1)
    sub = lax.broadcasted_iota(jnp.int32, (8, LANES), 0)
    tiles = list(tiles)
    count = len(tiles)
    for first in range(0, count, GROUP):
        last = min(first + GROUP, count)
        ahead = None
        done = []
        for step in range(first, last):
            base = step * 8
            inside = (lane >= base) & (lane < base + 8)

            def columns(x, start):
                return [jnp.broadcast_to(x[:, start + c : start + c + 1], (8, LANES)) for c in range(8)]

            head = tiles[step]
            cols = columns(head, base) if ahead is None else ahead
            head = jnp.where(inside, jnp.where(sub == lane - base, 1.0, 0.0), head)
            pivots = jnp.ones((8, LANES), F32)
            pairs = []
            for r in (0, 2, 4, 6):
                q = r + 1
                a, b, c = spread(cols[r], r), spread(cols[q], r), spread(cols[q], q)
                det = a * c - b * b
                inv = 1.0 / det
                ai, bi, ci = a * inv, b * inv, c * inv
                u, v = cols[r], cols[q]
                below = sub > q
                alpha = jnp.where(below, u * ci - v * bi, 0.0)
                beta = jnp.where(below, v * ai - u * bi, 0.0)
                row_r, row_q = spread(head, r), spread(head, q)
                tops = {}
                for k in range(q + 1, 8):
                    tops[k] = (spread(cols[k], r), spread(cols[k], q))
                    cols[k] = cols[k] - alpha * tops[k][0] - beta * tops[k][1]
                ainv = 1.0 / a
                head = head - (alpha + jnp.where(sub == q, b * ainv, 0.0)) * row_r - beta * row_q
                pivots = jnp.where(sub == r, a, jnp.where(sub == q, det * ainv, pivots))
                pairs.append((r, ai, bi, ci, row_r, row_q, tops))
            scaled = head * lax.rsqrt(pivots)
            own = lane <= base + sub
            tiles[step] = jnp.where(own, scaled, 0.0)
            done.append((scaled, jnp.where(own | (lane >= last * 8), scaled, 0.0)))
            ahead = None
            for m in range(step + 1, last):
                tile = tiles[m]
                cols = columns(tile, base)
                if m == step + 1:
                    ahead = columns(tile, base + 8)
                tile = jnp.where(inside, 0.0, tile)
                for r, ai, bi, ci, row_r, row_q, tops in pairs:
                    u, v = cols[r], cols[r + 1]
                    alpha = u * ci - v * bi
                    beta = v * ai - u * bi
                    tile = tile - alpha * row_r - beta * row_q
                    for k in tops:
                        cols[k] = cols[k] - alpha * tops[k][0] - beta * tops[k][1]
                    if m == step + 1:
                        for c in range(8):
                            ahead[c] = ahead[c] - alpha * spread(u, c) - beta * spread(v, c)
                tiles[m] = tile
        if last < count:
            far = lane >= 8 * last
            keep = far | (lane < 8 * first)
            left = three_parts(jnp.concatenate([jnp.where(far, x, 0.0) for x, _ in done], axis=0))
            right = three_parts(jnp.concatenate([y for _, y in done], axis=0))
            left = jnp.concatenate([left[k] for k in (0, 0, 1, 0, 1, 2)], axis=0).astype(BF16)
            right = jnp.concatenate([right[k] for k in (0, 1, 0, 2, 1, 0)], axis=0).astype(BF16)
            update = lax.dot_general(left, right, (((0,), (0,)), ((), ())), preferred_element_type=F32)
            for m in range(last, count):
                tiles[m] = jnp.where(keep, tiles[m], 0.0) - update[8 * m : 8 * m + 8]
    return tiles


def split_parts(x):
    return [part.astype(BF16) for part in three_parts(x)]


def stacked(a, parts, side=0):
    n = a.shape[0]
    rows = jnp.concatenate(split_parts(a), axis=0)
    first, second, third = [
        lax.dot_general(rows[: (3 - k) * n], part, (((1,), (side,)), ((), ())), preferred_element_type=F32)
        for k, part in enumerate(parts)
    ]
    small = first[2 * n :] + second[n:] + third
    return first[:n] + (first[n : 2 * n] + second[:n] + small)


def factor_block(block):
    tiles = [block[8 * m : 8 * m + 8, :] for m in range(block.shape[0] // 8)]
    return jnp.concatenate(inverse_factor(tiles), axis=0)


def widen(x, width):
    return jnp.concatenate([x, jnp.zeros((x.shape[0], width - x.shape[1]), x.dtype)], axis=1)


def unpack(sums, start):
    r = lax.broadcasted_iota(jnp.int32, (LANES, LANES), 0)
    c = lax.broadcasted_iota(jnp.int32, (LANES, LANES), 1)
    part = lambda first, rows: sums[pl.ds(start + first, rows), :]
    square = part(SQUARE, LANES)
    turned = square.T
    corner = jnp.where(r >= c, square, turned)
    second = jnp.where(r == c, part(LAST + 47, 1), jnp.where(r < c, square, turned))
    blocks = [
        (corner, part(BELOW[0], USED - 128)),
        (second, part(BELOW[1], USED - 256)),
        (part(THIRD, LANES), part(BELOW[2], USED - 384)),
    ]
    return [jnp.concatenate(pair, axis=0) for pair in blocks] + [part(LAST, USED - 384)]


def fill_unit(block):
    r = lax.broadcasted_iota(jnp.int32, block.shape, 0)
    c = lax.broadcasted_iota(jnp.int32, block.shape, 1)
    return jnp.where((r >= VALID - 384) | (c >= VALID - 384), jnp.where(r == c, 1.0, 0.0), block)


def finish_kernel(side_ref, mine_ref, other_ref, pick_ref, start_ref, out_ref, sums, signal, inverse):
    side = side_ref[0]
    sums[pl.ds(pl.multiple_of(side * PACKED, 8), PACKED), :] = mine_ref[...]
    sums[pl.ds(pl.multiple_of((1 - side) * PACKED, 8), PACKED), :] = other_ref[...]

    signal[...] = jnp.zeros_like(signal)
    panels = unpack(sums, PACKED)
    panels[3] = fill_unit(panels[3])
    for panel in range(4):
        low = panel * LANES
        signal[low:USED, low : low + LANES] = panels[panel]
        for other in range(panel + 1, 4):
            first = other * LANES
            size = min(LANES, USED - first)
            signal[low : low + LANES, first : first + size] = panels[panel][first - low : first - low + size].T
    basis = mm(start_ref[...], pick_ref[...].astype(F32), ((0,), (0,)))[:, :USED]

    total = 64.0 * sums[LAST + 46 : LAST + 47, :]
    panels = [block / total for block in unpack(sums, 0)]
    panels[3] = fill_unit(panels[3])
    inverse[...] = jnp.zeros_like(inverse)
    known = None
    for j in range(4):
        low = j * LANES
        size = min(LANES, USED - low)
        own = factor_block(panels[j][:size])
        inverse[low : low + size, low : low + LANES] = own
        if j == 3:
            inverse[low:USED, :low] = -mm(own[:, :size], known)
            break
        below = mm(panels[j][LANES:], own, ((1,), (1,)))
        for k in range(j + 1, 4):
            skip = (k - j - 1) * LANES
            width = min(LANES, USED - k * LANES)
            update = mm(below[skip:], below[skip : skip + width], ((1,), (1,)))
            panels[k] = panels[k] - (update if width == LANES else widen(update, LANES))
        gain = mm(below, own)
        if j == 0:
            known = gain
        else:
            left = -mm(own, known[:LANES])
            inverse[low : low + LANES, :low] = left
            known = jnp.concatenate([known[LANES:] + mm(below, left), gain], axis=1)

    inverse_parts = split_parts(inverse[...])
    signal_parts = split_parts(signal[...])
    turned = stacked(basis, inverse_parts)
    mapped = stacked(stacked(turned[:, :USED], signal_parts), inverse_parts, 1)
    for sweep in range(SWEEPS):
        square = mm(mapped, mapped, ((1,), (1,)))
        turned = stacked(mapped, inverse_parts)
        if sweep + 1 < SWEEPS:
            ahead = stacked(stacked(turned[:, :USED], signal_parts), inverse_parts, 1)
        scale = factor_block(square)
        if sweep + 1 < SWEEPS:
            mapped = mm(scale, ahead)
    weights = mm(scale, turned).astype(BF16)
    out_ref[...] = lax.dot_general(
        pick_ref[...], weights, (((1,), (1,)), ((), ())), preferred_element_type=F32
    ).astype(BF16)


def finish(side, mine, other, pick, start_basis):
    vmem = pl.BlockSpec(memory_space=pltpu.VMEM)
    return pl.pallas_call(
        finish_kernel,
        out_shape=jax.ShapeDtypeStruct((512, LANES), BF16),
        in_specs=[pl.BlockSpec(memory_space=pltpu.SMEM)] + [vmem] * 4,
        out_specs=vmem,
        scratch_shapes=[
            pltpu.VMEM((2 * PACKED, LANES), F32),
            pltpu.VMEM((USED, 512), F32),
            pltpu.VMEM((USED, 512), F32),
        ],
        compiler_params=pltpu.CompilerParams(vmem_limit_bytes=20 << 20),
    )(side, mine, other, pick, start_basis)


def local(radiance, band_mask, row_counts, noise_kernel, smooth_kernel, start_basis):
    height, across, bands = radiance.shape
    count = row_counts[0]
    chain = 1
    for axis in AXES:
        chain *= lax.axis_size(axis)
    up = [(i, i + 1) for i in range(chain - 1)]
    row = jnp.arange(height, dtype=jnp.int32)
    zero = jnp.zeros((), radiance.dtype)
    flat = radiance.reshape(height * across, bands)
    tail = jnp.where((row[-4:] < count)[:, None, None], radiance[-4:], zero).reshape(4 * across, bands)
    tail = jnp.concatenate([tail, jnp.full((16, bands), count, radiance.dtype)], axis=0)
    low = lax.ppermute(tail, AXES, up)

    noise, signal, pick, taps = inner(row_counts, band_mask[None], noise_kernel, smooth_kernel, flat)
    side = lax.axis_index("sub")
    place_in_chain = lax.axis_index(AXES)
    state = jnp.stack([count, side, place_in_chain == 0, place_in_chain == chain - 1]).astype(jnp.int32)
    keep, send = edge(state, low, flat, pick, taps, noise, signal)
    mine, other = total_sum(keep, send)
    weights = finish(state[1:2], mine, other, pick, start_basis)
    keep = jnp.repeat(row < count, across)
    masked = jnp.where(keep[:, None], flat, zero)
    result = jnp.dot(masked, weights, preferred_element_type=F32)
    return result.reshape(height, across, weights.shape[1])


def solution(mesh):
    split = P(("groups",) + AXES)
    return jax.shard_map(
        local,
        mesh=mesh,
        in_specs=(P(("groups",) + AXES, None, None), P(), split, P(), P(), P()),
        out_specs=P(("groups",) + AXES, None, None),
        check_vma=False,
    )
```

```python
import jax
import jax.numpy as jnp
from jax import lax
from jax.experimental import pallas as pl
from jax.experimental.pallas import tpu as pltpu
from jax.sharding import PartitionSpec as P

SWEEPS = 2
VALID = 425
AXES = ("wide", "narrow", "sub")
LANES = 128
USED = 432
PACKED = 832
SQUARE, THIRD, LAST = 0, 128, 256
BELOW = (304, 608, 784)
PITCH = 72
GROUP = 8
HIGH = lax.Precision.HIGHEST
F32 = jnp.float32
BF16 = jnp.bfloat16


def mm(a, b, dims=((1,), (0,))):
    return lax.dot_general(a, b, (dims, ((), ())), precision=HIGH, preferred_element_type=F32)


def place(xs, values, rows, slot, row, limit):
    pitch = xs.shape[0] // 4
    for k in range(rows):
        piece = values[k * 64 : (k + 1) * 64]
        if limit is not None:
            piece = jnp.where(row + k < limit, piece, 0.0)
        start = pl.multiple_of(8 + (slot + k) * PITCH, 8)
        for tile in range(4):
            xs[pl.ds(start + tile * pitch, 64), :] = piece[:, tile * LANES : (tile + 1) * LANES]


def clear_gaps(xs, slots):
    pitch = xs.shape[0] // 4
    zeros = jnp.zeros((8, LANES), F32)
    for tile in range(4):
        for slot in range(slots + 1):
            start = tile * pitch + slot * PITCH
            xs[start : start + 8, :] = zeros


def noise_tile(xs, taps, slot, valid, tile):
    pitch = xs.shape[0] // 4
    lanes = slice(tile * LANES, (tile + 1) * LANES)
    tap = lambda k: taps[k : k + 1, lanes]
    even = odd = None
    for row_off in (-1, 0, 1):
        base = tile * pitch + 8 + (slot + row_off) * PITCH
        here_even = xs[pl.ds(base, 32, stride=2), :]
        next_even = xs[pl.ds(base + 2, 32, stride=2), :]
        prev_odd = xs[pl.ds(base - 1, 32, stride=2), :]
        here_odd = xs[pl.ds(base + 1, 32, stride=2), :]
        if row_off == 0:
            left, right = tap(3), tap(4)
            part_even = here_even - left * prev_odd - right * here_odd
            part_odd = here_odd - left * here_even - right * next_even
        else:
            first = 0 if row_off == -1 else 5
            left, mid, right = tap(first), tap(first + 1), tap(first + 2)
            part_even = -(left * prev_odd + mid * here_even + right * here_odd)
            part_odd = -(left * here_even + mid * here_odd + right * next_even)
        even = part_even if even is None else even + part_even
        odd = part_odd if odd is None else odd + part_odd
    return jnp.where(valid, even, 0.0).astype(BF16), jnp.where(valid, odd, 0.0).astype(BF16)


def signal_tile(xs, taps, slot, tile, valid=None):
    pitch = xs.shape[0] // 4
    lanes = slice(tile * LANES, (tile + 1) * LANES)
    total = None
    for i in range(5):
        base = tile * pitch + 8 + (slot + i) * PITCH
        for j in range(5):
            k = 8 + 5 * i + j
            term = taps[k : k + 1, lanes] * xs[pl.ds(base + j - 2, 32, stride=2), :]
            total = term if total is None else total + term
    if valid is not None:
        total = jnp.where(valid, total, 0.0)
    return total.astype(BF16)


def panel_grams(field):
    return [
        lax.dot_general(
            field[:, low:], field[:, low : low + LANES], (((0,), (0,)), ((), ())), preferred_element_type=F32
        )
        for low in range(0, 4 * LANES, LANES)
    ]


def packed(panels):
    r = lax.broadcasted_iota(jnp.int32, (LANES, LANES), 0)
    c = lax.broadcasted_iota(jnp.int32, (LANES, LANES), 1)
    corners = [block[:LANES] for block in panels]
    blocks = [(BELOW[k], panels[k][LANES : USED - k * LANES]) for k in range(3)]
    blocks.append((SQUARE, jnp.where(r >= c, corners[0], corners[1])))
    blocks.append((THIRD, corners[2]))
    diagonal = jnp.sum(jnp.where(r == c, corners[1], 0.0), axis=0, keepdims=True)
    tail = corners[3][: USED - 384]
    row = lax.broadcasted_iota(jnp.int32, tail.shape, 0)
    blocks.append((LAST, jnp.where(row == 47, diagonal, tail)))
    return blocks


def inner_kernel(
    count_ref, mask_hbm, noise_hbm, smooth_hbm, x_hbm, noise_out, signal_out, pick_ref, taps,
    x, xs, nf, sg, sums, mask_ref, noise_ref, smooth_ref, sems, small_sems,
):
    height = x.shape[0] // 64
    bands = x.shape[1]
    chunks = sems.shape[0]
    size = x.shape[0] // chunks
    copies = [
        pltpu.make_async_copy(x_hbm.at[pl.ds(k * size, size)], x.at[pl.ds(k * size, size)], sems.at[k])
        for k in range(chunks)
    ]
    small = [
        pltpu.make_async_copy(source, target, small_sems.at[k])
        for k, (source, target) in enumerate(
            ((mask_hbm, mask_ref), (noise_hbm, noise_ref), (smooth_hbm, smooth_ref))
        )
    ]
    for copy in small + copies:
        copy.start()
    clear_gaps(xs, height)
    for copy in small:
        copy.wait()
    count = count_ref[0]
    mask = jnp.broadcast_to(mask_ref[...].astype(F32), (16, bands)).astype(BF16)
    r = lax.broadcasted_iota(jnp.int32, (bands, bands), 0)
    c = lax.broadcasted_iota(jnp.int32, (bands, bands), 1)
    ranks = jnp.where(c < r, 1.0, jnp.where(c == r, 1024.0, 0.0)).astype(BF16)
    position = lax.dot_general(ranks, mask, (((1,), (1,)), ((), ())), preferred_element_type=F32)[:, :1]
    pick_ref[...] = jnp.where(position == (c + 1024).astype(F32), 1.0, 0.0).astype(BF16)
    pick = pick_ref[...]
    weights = jnp.concatenate([noise_ref[...], smooth_ref[...], jnp.zeros((7, bands), F32)], axis=0)
    weights = jnp.concatenate(three_parts(weights), axis=0).astype(BF16)
    weights = jnp.dot(weights, pick, preferred_element_type=F32)
    taps[...] = weights[:40] + (weights[40:80] + weights[80:])
    for copy in copies:
        copy.wait()

    def picked(k):
        return jnp.dot(x[pl.ds(pl.multiple_of(k * 256, 256), 256), :], pick, preferred_element_type=F32)

    def noise_row(row):
        start = pl.multiple_of((row + 1) * 64, 64)
        for tile in range(4):
            lanes = slice(tile * LANES, (tile + 1) * LANES)
            even, odd = noise_tile(xs, taps, row, row < count, tile)
            nf[pl.ds(start, 32), lanes] = even
            nf[pl.ds(start + 32, 32), lanes] = odd

    def add_gram(k):
        chunk = nf[pl.ds(pl.multiple_of(k * 256, 256), 256), :]
        for panel in range(4):
            low = panel * LANES
            sums[panel, low:, :] += lax.dot_general(
                chunk[:, low:], chunk[:, low : low + LANES], (((0,), (0,)), ((), ())), preferred_element_type=F32
            )

    groups = height // 4
    place(xs, picked(0), 4, 0, 0, count)
    place(xs, picked(1), 4, 4, 4, count)
    sums[...] = jnp.zeros_like(sums)
    nf[:128, :] = jnp.zeros((128, bands), BF16)
    noise_row(1)
    noise_row(2)

    def body(k, carry):
        following = jnp.minimum(k + 1, groups - 1)
        values = picked(following)
        add_gram(k - 1)
        for row in range(4):
            noise_row(4 * k - 1 + row)
        for half in range(2):
            slot = 4 * k - 4 + 2 * half
            start = pl.multiple_of((2 * k - 2 + half) * 32, 32)
            for tile in range(4):
                sg[pl.ds(start, 32), tile * LANES : (tile + 1) * LANES] = signal_tile(xs, taps, slot, tile)
        place(xs, values, 4, following * 4, following * 4, count)
        return carry

    lax.fori_loop(1, groups, body, 0)
    add_gram(groups - 1)
    corners = [[sums[panel, panel * LANES :, :] for panel in range(4)], panel_grams(sg)]
    for panels, out_ref in zip(corners, (noise_out, signal_out)):
        for start, block in packed(panels):
            out_ref[start : start + block.shape[0], :] = block


def edge_kernel(
    state_ref, low_hbm, x_hbm, pick_ref, taps, noise_ref, signal_ref, keep_ref, send_ref, rows, both, xs, nf, sg, sems
):
    count, side, first, last = [state_ref[k] for k in range(4)]
    size = x_hbm.shape[0]
    height = size // 64
    pieces = ((low_hbm, 0, 272), (x_hbm.at[pl.ds(0, 192)], 272, 192), (x_hbm.at[pl.ds(size - 256, 256)], 464, 256))
    copies = [
        pltpu.make_async_copy(source, rows.at[pl.ds(start, length)], sems.at[k])
        for k, (source, start, length) in enumerate(pieces)
    ]
    for copy in copies:
        copy.start()
    pick = pick_ref[...]
    clear_gaps(xs, 12)
    pitch = xs.shape[0] // 4
    for tile in range(4):
        start = tile * pitch + 8 + 11 * PITCH
        xs[start : start + 64, :] = jnp.zeros((64, LANES), F32)
    for copy in copies:
        copy.wait()
    values = jnp.dot(rows[...], pick, preferred_element_type=F32)
    place(xs, values[:256], 4, 0, 0, None)
    place(xs, values[272:464], 3, 4, 0, count)
    place(xs, values[464:], 4, 7, height - 4, count)
    before = jnp.broadcast_to(rows[256:272, :LANES].astype(F32)[:1], (32, LANES))
    noise_rows = ((3, before > float(height - 1)), (4, count > 0), (10, (last == 1) & (count > height - 1)))
    signal_rows = ((0, first == 0), (2, None), (7, last == 1))
    for tile in range(4):
        lanes = slice(tile * LANES, (tile + 1) * LANES)
        for k, (slot, valid) in enumerate(noise_rows):
            even, odd = noise_tile(xs, taps, slot, valid, tile)
            nf[k * 64 : k * 64 + 32, lanes] = even
            nf[k * 64 + 32 : k * 64 + 64, lanes] = odd
        for k, (slot, valid) in enumerate(signal_rows):
            sg[k * 32 : k * 32 + 32, lanes] = signal_tile(xs, taps, slot, tile, valid)
    for half, (field, inner) in enumerate(((nf, noise_ref), (sg, signal_ref))):
        for start, block in packed(panel_grams(field)):
            length = block.shape[0]
            block = block + inner[start : start + length, :]
            if start == LAST:
                row = lax.broadcasted_iota(jnp.int32, block.shape, 0)
                block = jnp.where(row == 46, count.astype(F32), block)
            both[half * PACKED + start : half * PACKED + start + length, :] = block
    keep_ref[...] = both[pl.ds(pl.multiple_of(side * PACKED, 8), PACKED), :]
    send_ref[...] = both[pl.ds(pl.multiple_of((1 - side) * PACKED, 8), PACKED), :]


VMEM = pl.BlockSpec(memory_space=pltpu.VMEM)
SMEM = pl.BlockSpec(memory_space=pltpu.SMEM)
HBM = pl.BlockSpec(memory_space=pltpu.HBM)
PARAMS = pltpu.CompilerParams(vmem_limit_bytes=20 << 20)


def inner(count, mask, noise_kernel, smooth_kernel, x):
    height, bands = x.shape[0] // 64, x.shape[1]
    gram = jax.ShapeDtypeStruct((PACKED, LANES), F32)
    return pl.pallas_call(
        inner_kernel,
        out_shape=(gram, gram, jax.ShapeDtypeStruct((bands, bands), BF16), jax.ShapeDtypeStruct((40, bands), F32)),
        in_specs=[SMEM] + [HBM] * 4,
        out_specs=(VMEM,) * 4,
        scratch_shapes=[
            pltpu.VMEM(x.shape, BF16),
            pltpu.VMEM((4 * (16 + height * PITCH), LANES), F32),
            pltpu.VMEM((height * 64, bands), BF16),
            pltpu.VMEM(((height // 2 - 2) * 32, bands), BF16),
            pltpu.VMEM((4, bands, LANES), F32),
            pltpu.VMEM(mask.shape, jnp.int32),
            pltpu.VMEM(noise_kernel.shape, F32),
            pltpu.VMEM(smooth_kernel.shape, F32),
            pltpu.SemaphoreType.DMA((8,)),
            pltpu.SemaphoreType.DMA((3,)),
        ],
        compiler_params=PARAMS,
        cost_estimate=pl.CostEstimate(flops=6 << 30, transcendentals=0, bytes_accessed=8 << 20),
        name="inner",
    )(count, *(pltpu.with_memory_space_constraint(a, pltpu.HBM) for a in (mask, noise_kernel, smooth_kernel, x)))


def edge(state, low, x, pick, taps, noise, signal):
    bands = x.shape[1]
    gram = jax.ShapeDtypeStruct((PACKED, LANES), F32)
    return pl.pallas_call(
        edge_kernel,
        out_shape=(gram, gram),
        in_specs=[SMEM, pl.BlockSpec(memory_space=pl.ANY), HBM, VMEM, VMEM, VMEM, VMEM],
        out_specs=(VMEM, VMEM),
        scratch_shapes=[
            pltpu.VMEM((720, bands), BF16),
            pltpu.VMEM((2 * PACKED, LANES), F32),
            pltpu.VMEM((4 * (16 + 12 * PITCH), LANES), F32),
            pltpu.VMEM((192, bands), BF16),
            pltpu.VMEM((96, bands), BF16),
            pltpu.SemaphoreType.DMA((3,)),
        ],
        compiler_params=PARAMS,
        name="edge",
    )(state, low, pltpu.with_memory_space_constraint(x, pltpu.HBM), pick, taps, noise, signal)


def scatter_sum(parts, axis):
    n = lax.axis_size(axis)
    me = lax.axis_index(axis)

    def block(k):
        return [lax.dynamic_index_in_dim(x.reshape(n, -1, LANES), k, 0, keepdims=False) for x in parts]

    got = []
    for d in range(1, n):
        got.append(lax.ppermute(sum(block((me + d) % n)), axis, [(i, (i + d) % n) for i in range(n)]))
    return block(me) + got


def gather_rows(x, axis):
    n = lax.axis_size(axis)
    me = lax.axis_index(axis)
    got = [x] + [lax.ppermute(x, axis, [(i, (i + d) % n) for i in range(n)]) for d in range(1, n)]
    if n == 2:
        return jnp.concatenate([jnp.where(me == 0, got[0], got[1]), jnp.where(me == 0, got[1], got[0])])
    stacked = jnp.stack(got)
    return jnp.concatenate([lax.dynamic_index_in_dim(stacked, (me - j) % n, 0, keepdims=False) for j in range(n)])


def exchange(x):
    return lax.ppermute(x, "sub", [(0, 1), (1, 0)])


def total_sum(keep, send):
    parts = [keep, exchange(send)]
    short = [axis for axis in ("wide", "narrow") if lax.axis_size(axis) <= 4]
    long = tuple(axis for axis in ("wide", "narrow") if axis not in short)
    for axis in short:
        parts = scatter_sum(parts, axis)
    x = sum(parts)
    if long:
        x = lax.psum(x, long)
    for axis in reversed(short):
        x = gather_rows(x, axis)
    return x, exchange(x)


def spread(x, row):
    return jnp.broadcast_to(x[row : row + 1, :], (8, LANES))


def three_parts(x):
    high = x.astype(BF16).astype(F32)
    rest = x - high
    mid = rest.astype(BF16).astype(F32)
    return high, mid, rest - mid


def inverse_factor(tiles):
    lane = lax.broadcasted_iota(jnp.int32, (8, LANES), 1)
    sub = lax.broadcasted_iota(jnp.int32, (8, LANES), 0)
    tiles = list(tiles)
    count = len(tiles)
    for first in range(0, count, GROUP):
        last = min(first + GROUP, count)
        ahead = None
        done = []
        for step in range(first, last):
            base = step * 8
            inside = (lane >= base) & (lane < base + 8)

            def columns(x, start):
                return [jnp.broadcast_to(x[:, start + c : start + c + 1], (8, LANES)) for c in range(8)]

            head = tiles[step]
            cols = columns(head, base) if ahead is None else ahead
            head = jnp.where(inside, jnp.where(sub == lane - base, 1.0, 0.0), head)
            pivots = jnp.ones((8, LANES), F32)
            pairs = []
            for r in (0, 2, 4, 6):
                q = r + 1
                a, b, c = spread(cols[r], r), spread(cols[q], r), spread(cols[q], q)
                det = a * c - b * b
                inv = 1.0 / det
                ai, bi, ci = a * inv, b * inv, c * inv
                u, v = cols[r], cols[q]
                below = sub > q
                alpha = jnp.where(below, u * ci - v * bi, 0.0)
                beta = jnp.where(below, v * ai - u * bi, 0.0)
                row_r, row_q = spread(head, r), spread(head, q)
                tops = {}
                for k in range(q + 1, 8):
                    tops[k] = (spread(cols[k], r), spread(cols[k], q))
                    cols[k] = cols[k] - alpha * tops[k][0] - beta * tops[k][1]
                ainv = 1.0 / a
                head = head - (alpha + jnp.where(sub == q, b * ainv, 0.0)) * row_r - beta * row_q
                pivots = jnp.where(sub == r, a, jnp.where(sub == q, det * ainv, pivots))
                pairs.append((r, ai, bi, ci, row_r, row_q, tops))
            scaled = head * lax.rsqrt(pivots)
            own = lane <= base + sub
            tiles[step] = jnp.where(own, scaled, 0.0)
            done.append((scaled, jnp.where(own | (lane >= last * 8), scaled, 0.0)))
            ahead = None
            for m in range(step + 1, last):
                tile = tiles[m]
                cols = columns(tile, base)
                if m == step + 1:
                    ahead = columns(tile, base + 8)
                tile = jnp.where(inside, 0.0, tile)
                for r, ai, bi, ci, row_r, row_q, tops in pairs:
                    u, v = cols[r], cols[r + 1]
                    alpha = u * ci - v * bi
                    beta = v * ai - u * bi
                    tile = tile - alpha * row_r - beta * row_q
                    for k in tops:
                        cols[k] = cols[k] - alpha * tops[k][0] - beta * tops[k][1]
                    if m == step + 1:
                        for c in range(8):
                            ahead[c] = ahead[c] - alpha * spread(u, c) - beta * spread(v, c)
                tiles[m] = tile
        if last < count:
            far = lane >= 8 * last
            keep = far | (lane < 8 * first)
            left = three_parts(jnp.concatenate([jnp.where(far, x, 0.0) for x, _ in done], axis=0))
            right = three_parts(jnp.concatenate([y for _, y in done], axis=0))
            left = jnp.concatenate([left[k] for k in (0, 0, 1, 0, 1, 2)], axis=0).astype(BF16)
            right = jnp.concatenate([right[k] for k in (0, 1, 0, 2, 1, 0)], axis=0).astype(BF16)
            update = lax.dot_general(left, right, (((0,), (0,)), ((), ())), preferred_element_type=F32)
            for m in range(last, count):
                tiles[m] = jnp.where(keep, tiles[m], 0.0) - update[8 * m : 8 * m + 8]
    return tiles


def split_parts(x):
    return [part.astype(BF16) for part in three_parts(x)]


def stacked(a, parts, side=0):
    n = a.shape[0]
    rows = jnp.concatenate(split_parts(a), axis=0)
    first, second, third = [
        lax.dot_general(rows[: (3 - k) * n], part, (((1,), (side,)), ((), ())), preferred_element_type=F32)
        for k, part in enumerate(parts)
    ]
    small = first[2 * n :] + second[n:] + third
    return first[:n] + (first[n : 2 * n] + second[:n] + small)


def factor_block(block):
    tiles = [block[8 * m : 8 * m + 8, :] for m in range(block.shape[0] // 8)]
    return jnp.concatenate(inverse_factor(tiles), axis=0)


def widen(x, width):
    return jnp.concatenate([x, jnp.zeros((x.shape[0], width - x.shape[1]), x.dtype)], axis=1)


def unpack(sums, start):
    r = lax.broadcasted_iota(jnp.int32, (LANES, LANES), 0)
    c = lax.broadcasted_iota(jnp.int32, (LANES, LANES), 1)
    part = lambda first, rows: sums[pl.ds(start + first, rows), :]
    square = part(SQUARE, LANES)
    turned = square.T
    corner = jnp.where(r >= c, square, turned)
    second = jnp.where(r == c, part(LAST + 47, 1), jnp.where(r < c, square, turned))
    blocks = [
        (corner, part(BELOW[0], USED - 128)),
        (second, part(BELOW[1], USED - 256)),
        (part(THIRD, LANES), part(BELOW[2], USED - 384)),
    ]
    return [jnp.concatenate(pair, axis=0) for pair in blocks] + [part(LAST, USED - 384)]


def fill_unit(block):
    r = lax.broadcasted_iota(jnp.int32, block.shape, 0)
    c = lax.broadcasted_iota(jnp.int32, block.shape, 1)
    return jnp.where((r >= VALID - 384) | (c >= VALID - 384), jnp.where(r == c, 1.0, 0.0), block)


def finish_kernel(side_ref, mine_ref, other_ref, pick_ref, start_ref, out_ref, sums, signal, inverse):
    side = side_ref[0]
    sums[pl.ds(pl.multiple_of(side * PACKED, 8), PACKED), :] = mine_ref[...]
    sums[pl.ds(pl.multiple_of((1 - side) * PACKED, 8), PACKED), :] = other_ref[...]

    signal[...] = jnp.zeros_like(signal)
    panels = unpack(sums, PACKED)
    panels[3] = fill_unit(panels[3])
    for panel in range(4):
        low = panel * LANES
        signal[low:USED, low : low + LANES] = panels[panel]
        for other in range(panel + 1, 4):
            first = other * LANES
            size = min(LANES, USED - first)
            signal[low : low + LANES, first : first + size] = panels[panel][first - low : first - low + size].T
    basis = mm(start_ref[...], pick_ref[...].astype(F32), ((0,), (0,)))[:, :USED]

    total = 64.0 * sums[LAST + 46 : LAST + 47, :]
    panels = [block / total for block in unpack(sums, 0)]
    panels[3] = fill_unit(panels[3])
    inverse[...] = jnp.zeros_like(inverse)
    known = None
    for j in range(4):
        low = j * LANES
        size = min(LANES, USED - low)
        own = factor_block(panels[j][:size])
        inverse[low : low + size, low : low + LANES] = own
        if j == 3:
            inverse[low:USED, :low] = -mm(own[:, :size], known)
            break
        below = mm(panels[j][LANES:], own, ((1,), (1,)))
        for k in range(j + 1, 4):
            skip = (k - j - 1) * LANES
            width = min(LANES, USED - k * LANES)
            update = mm(below[skip:], below[skip : skip + width], ((1,), (1,)))
            panels[k] = panels[k] - (update if width == LANES else widen(update, LANES))
        gain = mm(below, own)
        if j == 0:
            known = gain
        else:
            left = -mm(own, known[:LANES])
            inverse[low : low + LANES, :low] = left
            known = jnp.concatenate([known[LANES:] + mm(below, left), gain], axis=1)

    inverse_parts = split_parts(inverse[...])
    signal_parts = split_parts(signal[...])
    turned = stacked(basis, inverse_parts)
    mapped = stacked(stacked(turned[:, :USED], signal_parts), inverse_parts, 1)
    for sweep in range(SWEEPS):
        square = mm(mapped, mapped, ((1,), (1,)))
        turned = stacked(mapped, inverse_parts)
        if sweep + 1 < SWEEPS:
            ahead = stacked(stacked(turned[:, :USED], signal_parts), inverse_parts, 1)
        scale = factor_block(square)
        if sweep + 1 < SWEEPS:
            mapped = mm(scale, ahead)
    weights = mm(scale, turned).astype(BF16)
    out_ref[...] = lax.dot_general(
        pick_ref[...], weights, (((1,), (1,)), ((), ())), preferred_element_type=F32
    ).astype(BF16)


def finish(side, mine, other, pick, start_basis):
    vmem = pl.BlockSpec(memory_space=pltpu.VMEM)
    return pl.pallas_call(
        finish_kernel,
        out_shape=jax.ShapeDtypeStruct((512, LANES), BF16),
        in_specs=[pl.BlockSpec(memory_space=pltpu.SMEM)] + [vmem] * 4,
        out_specs=vmem,
        scratch_shapes=[
            pltpu.VMEM((2 * PACKED, LANES), F32),
            pltpu.VMEM((USED, 512), F32),
            pltpu.VMEM((USED, 512), F32),
        ],
        compiler_params=pltpu.CompilerParams(vmem_limit_bytes=20 << 20),
    )(side, mine, other, pick, start_basis)


def local(radiance, band_mask, row_counts, noise_kernel, smooth_kernel, start_basis):
    height, across, bands = radiance.shape
    count = row_counts[0]
    chain = 1
    for axis in AXES:
        chain *= lax.axis_size(axis)
    up = [(i, i + 1) for i in range(chain - 1)]
    row = jnp.arange(height, dtype=jnp.int32)
    zero = jnp.zeros((), radiance.dtype)
    flat = radiance.reshape(height * across, bands)
    tail = jnp.where((row[-4:] < count)[:, None, None], radiance[-4:], zero).reshape(4 * across, bands)
    tail = jnp.concatenate([tail, jnp.full((16, bands), count, radiance.dtype)], axis=0)
    low = lax.ppermute(tail, AXES, up)

    noise, signal, pick, taps = inner(row_counts, band_mask[None], noise_kernel, smooth_kernel, flat)
    side = lax.axis_index("sub")
    place_in_chain = lax.axis_index(AXES)
    state = jnp.stack([count, side, place_in_chain == 0, place_in_chain == chain - 1]).astype(jnp.int32)
    keep, send = edge(state, low, flat, pick, taps, noise, signal)
    mine, other = total_sum(keep, send)
    weights = finish(state[1:2], mine, other, pick, start_basis)
    keep = jnp.repeat(row < count, across)
    masked = jnp.where(keep[:, None], flat, zero)
    result = jnp.dot(masked, weights, preferred_element_type=F32)
    return result.reshape(height, across, weights.shape[1])


def solution(mesh):
    split = P(("groups",) + AXES)
    return jax.shard_map(
        local,
        mesh=mesh,
        in_specs=(P(("groups",) + AXES, None, None), P(), split, P(), P(), P()),
        out_specs=P(("groups",) + AXES, None, None),
        check_vma=False,
    )
```

```python
import jax
import jax.numpy as jnp
from jax import lax
from jax.experimental import pallas as pl
from jax.experimental.pallas import tpu as pltpu
from jax.sharding import PartitionSpec as P

SWEEPS = 2
VALID = 425
AXES = ("wide", "narrow", "sub")
LANES = 128
USED = 432
PACKED = 832
SQUARE, THIRD, LAST = 0, 128, 256
BELOW = (304, 608, 784)
PITCH = 72
GROUP = 8
HIGH = lax.Precision.HIGHEST
F32 = jnp.float32
BF16 = jnp.bfloat16


def mm(a, b, dims=((1,), (0,))):
    return lax.dot_general(a, b, (dims, ((), ())), precision=HIGH, preferred_element_type=F32)


def place(xs, values, rows, slot, row, limit):
    pitch = xs.shape[0] // 4
    for k in range(rows):
        piece = values[k * 64 : (k + 1) * 64]
        if limit is not None:
            piece = jnp.where(row + k < limit, piece, 0.0)
        start = pl.multiple_of(8 + (slot + k) * PITCH, 8)
        for tile in range(4):
            xs[pl.ds(start + tile * pitch, 64), :] = piece[:, tile * LANES : (tile + 1) * LANES]


def clear_gaps(xs, slots):
    pitch = xs.shape[0] // 4
    zeros = jnp.zeros((8, LANES), F32)
    for tile in range(4):
        for slot in range(slots + 1):
            start = tile * pitch + slot * PITCH
            xs[start : start + 8, :] = zeros


def noise_tile(xs, taps, slot, valid, tile):
    pitch = xs.shape[0] // 4
    lanes = slice(tile * LANES, (tile + 1) * LANES)
    tap = lambda k: taps[k : k + 1, lanes]
    even = odd = None
    for row_off in (-1, 0, 1):
        base = tile * pitch + 8 + (slot + row_off) * PITCH
        here_even = xs[pl.ds(base, 32, stride=2), :]
        next_even = xs[pl.ds(base + 2, 32, stride=2), :]
        prev_odd = xs[pl.ds(base - 1, 32, stride=2), :]
        here_odd = xs[pl.ds(base + 1, 32, stride=2), :]
        if row_off == 0:
            left, right = tap(3), tap(4)
            part_even = here_even - left * prev_odd - right * here_odd
            part_odd = here_odd - left * here_even - right * next_even
        else:
            first = 0 if row_off == -1 else 5
            left, mid, right = tap(first), tap(first + 1), tap(first + 2)
            part_even = -(left * prev_odd + mid * here_even + right * here_odd)
            part_odd = -(left * here_even + mid * here_odd + right * next_even)
        even = part_even if even is None else even + part_even
        odd = part_odd if odd is None else odd + part_odd
    return jnp.where(valid, even, 0.0).astype(BF16), jnp.where(valid, odd, 0.0).astype(BF16)


def signal_tile(xs, taps, slot, tile, valid=None):
    pitch = xs.shape[0] // 4
    lanes = slice(tile * LANES, (tile + 1) * LANES)
    total = None
    for i in range(5):
        base = tile * pitch + 8 + (slot + i) * PITCH
        for j in range(5):
            k = 8 + 5 * i + j
            term = taps[k : k + 1, lanes] * xs[pl.ds(base + j - 2, 32, stride=2), :]
            total = term if total is None else total + term
    if valid is not None:
        total = jnp.where(valid, total, 0.0)
    return total.astype(BF16)


def panel_grams(field):
    return [
        lax.dot_general(
            field[:, low:], field[:, low : low + LANES], (((0,), (0,)), ((), ())), preferred_element_type=F32
        )
        for low in range(0, 4 * LANES, LANES)
    ]


def packed(panels):
    r = lax.broadcasted_iota(jnp.int32, (LANES, LANES), 0)
    c = lax.broadcasted_iota(jnp.int32, (LANES, LANES), 1)
    corners = [block[:LANES] for block in panels]
    blocks = [(BELOW[k], panels[k][LANES : USED - k * LANES]) for k in range(3)]
    blocks.append((SQUARE, jnp.where(r >= c, corners[0], corners[1])))
    blocks.append((THIRD, corners[2]))
    diagonal = jnp.sum(jnp.where(r == c, corners[1], 0.0), axis=0, keepdims=True)
    tail = corners[3][: USED - 384]
    row = lax.broadcasted_iota(jnp.int32, tail.shape, 0)
    blocks.append((LAST, jnp.where(row == 47, diagonal, tail)))
    return blocks


def inner_kernel(
    count_ref, mask_hbm, noise_hbm, smooth_hbm, x_hbm, noise_out, signal_out, pick_ref, taps, ends_ref,
    x, xs, nf, sg, sums, mask_ref, noise_ref, smooth_ref, sems, small_sems,
):
    height = x.shape[0] // 64
    bands = x.shape[1]
    chunks = sems.shape[0]
    size = x.shape[0] // chunks
    copies = [
        pltpu.make_async_copy(x_hbm.at[pl.ds(k * size, size)], x.at[pl.ds(k * size, size)], sems.at[k])
        for k in range(chunks)
    ]
    small = [
        pltpu.make_async_copy(source, target, small_sems.at[k])
        for k, (source, target) in enumerate(
            ((mask_hbm, mask_ref), (noise_hbm, noise_ref), (smooth_hbm, smooth_ref))
        )
    ]
    for copy in small + copies:
        copy.start()
    clear_gaps(xs, height)
    for copy in small:
        copy.wait()
    count = count_ref[0]
    mask = jnp.broadcast_to(mask_ref[...].astype(F32), (16, bands)).astype(BF16)
    r = lax.broadcasted_iota(jnp.int32, (bands, bands), 0)
    c = lax.broadcasted_iota(jnp.int32, (bands, bands), 1)
    ranks = jnp.where(c < r, 1.0, jnp.where(c == r, 1024.0, 0.0)).astype(BF16)
    position = lax.dot_general(ranks, mask, (((1,), (1,)), ((), ())), preferred_element_type=F32)[:, :1]
    pick_ref[...] = jnp.where(position == (c + 1024).astype(F32), 1.0, 0.0).astype(BF16)
    pick = pick_ref[...]
    weights = jnp.concatenate([noise_ref[...], smooth_ref[...], jnp.zeros((7, bands), F32)], axis=0)
    weights = jnp.concatenate(three_parts(weights), axis=0).astype(BF16)
    weights = jnp.dot(weights, pick, preferred_element_type=F32)
    taps[...] = weights[:40] + (weights[40:80] + weights[80:])
    for copy in copies:
        copy.wait()

    ends_ref[:192, :] = x[:192, :]
    ends_ref[192:, :] = x[x.shape[0] - 256 :, :]

    def picked(k):
        return jnp.dot(x[pl.ds(pl.multiple_of(k * 256, 256), 256), :], pick, preferred_element_type=F32)

    def noise_row(row):
        start = pl.multiple_of((row + 1) * 64, 64)
        for tile in range(4):
            lanes = slice(tile * LANES, (tile + 1) * LANES)
            even, odd = noise_tile(xs, taps, row, row < count, tile)
            nf[pl.ds(start, 32), lanes] = even
            nf[pl.ds(start + 32, 32), lanes] = odd

    def add_gram(k):
        chunk = nf[pl.ds(pl.multiple_of(k * 256, 256), 256), :]
        for panel in range(4):
            low = panel * LANES
            sums[panel, low:, :] += lax.dot_general(
                chunk[:, low:], chunk[:, low : low + LANES], (((0,), (0,)), ((), ())), preferred_element_type=F32
            )

    groups = height // 4
    place(xs, picked(0), 4, 0, 0, count)
    place(xs, picked(1), 4, 4, 4, count)
    sums[...] = jnp.zeros_like(sums)
    nf[:128, :] = jnp.zeros((128, bands), BF16)
    noise_row(1)
    noise_row(2)

    def body(k, carry):
        following = jnp.minimum(k + 1, groups - 1)
        values = picked(following)
        add_gram(k - 1)
        for row in range(4):
            noise_row(4 * k - 1 + row)
        for half in range(2):
            slot = 4 * k - 4 + 2 * half
            start = pl.multiple_of((2 * k - 2 + half) * 32, 32)
            for tile in range(4):
                sg[pl.ds(start, 32), tile * LANES : (tile + 1) * LANES] = signal_tile(xs, taps, slot, tile)
        place(xs, values, 4, following * 4, following * 4, count)
        return carry

    lax.fori_loop(1, groups, body, 0)
    add_gram(groups - 1)
    corners = [[sums[panel, panel * LANES :, :] for panel in range(4)], panel_grams(sg)]
    for panels, out_ref in zip(corners, (noise_out, signal_out)):
        for start, block in packed(panels):
            out_ref[start : start + block.shape[0], :] = block


def edge_kernel(
    state_ref, low_hbm, ends_ref, pick_ref, taps, noise_ref, signal_ref, keep_ref, send_ref, rows, both, xs, nf, sg, sems
):
    count, side, first, last, height = [state_ref[k] for k in range(5)]
    copy = pltpu.make_async_copy(low_hbm, rows, sems.at[0])
    copy.start()
    pick = pick_ref[...]
    clear_gaps(xs, 12)
    pitch = xs.shape[0] // 4
    for tile in range(4):
        start = tile * pitch + 8 + 11 * PITCH
        xs[start : start + 64, :] = jnp.zeros((64, LANES), F32)
    values = jnp.dot(ends_ref[...], pick, preferred_element_type=F32)
    place(xs, values[:192], 3, 4, 0, count)
    place(xs, values[192:], 4, 7, height - 4, count)
    copy.wait()
    place(xs, jnp.dot(rows[:256, :], pick, preferred_element_type=F32), 4, 0, 0, None)
    before = jnp.broadcast_to(rows[256:272, :LANES].astype(F32)[:1], (32, LANES))
    noise_rows = ((3, before > (height - 1).astype(F32)), (4, count > 0), (10, (last == 1) & (count > height - 1)))
    signal_rows = ((0, first == 0), (2, None), (7, last == 1))
    for tile in range(4):
        lanes = slice(tile * LANES, (tile + 1) * LANES)
        for k, (slot, valid) in enumerate(noise_rows):
            even, odd = noise_tile(xs, taps, slot, valid, tile)
            nf[k * 64 : k * 64 + 32, lanes] = even
            nf[k * 64 + 32 : k * 64 + 64, lanes] = odd
        for k, (slot, valid) in enumerate(signal_rows):
            sg[k * 32 : k * 32 + 32, lanes] = signal_tile(xs, taps, slot, tile, valid)
    for half, (field, inner) in enumerate(((nf, noise_ref), (sg, signal_ref))):
        for start, block in packed(panel_grams(field)):
            length = block.shape[0]
            block = block + inner[start : start + length, :]
            if start == LAST:
                row = lax.broadcasted_iota(jnp.int32, block.shape, 0)
                block = jnp.where(row == 46, count.astype(F32), block)
            both[half * PACKED + start : half * PACKED + start + length, :] = block
    keep_ref[...] = both[pl.ds(pl.multiple_of(side * PACKED, 8), PACKED), :]
    send_ref[...] = both[pl.ds(pl.multiple_of((1 - side) * PACKED, 8), PACKED), :]


VMEM = pl.BlockSpec(memory_space=pltpu.VMEM)
SMEM = pl.BlockSpec(memory_space=pltpu.SMEM)
HBM = pl.BlockSpec(memory_space=pltpu.HBM)
PARAMS = pltpu.CompilerParams(vmem_limit_bytes=20 << 20)


def inner(count, mask, noise_kernel, smooth_kernel, x):
    height, bands = x.shape[0] // 64, x.shape[1]
    gram = jax.ShapeDtypeStruct((PACKED, LANES), F32)
    return pl.pallas_call(
        inner_kernel,
        out_shape=(
            gram, gram, jax.ShapeDtypeStruct((bands, bands), BF16), jax.ShapeDtypeStruct((40, bands), F32),
            jax.ShapeDtypeStruct((448, bands), BF16),
        ),
        in_specs=[SMEM] + [HBM] * 4,
        out_specs=(VMEM,) * 5,
        scratch_shapes=[
            pltpu.VMEM(x.shape, BF16),
            pltpu.VMEM((4 * (16 + height * PITCH), LANES), F32),
            pltpu.VMEM((height * 64, bands), BF16),
            pltpu.VMEM(((height // 2 - 2) * 32, bands), BF16),
            pltpu.VMEM((4, bands, LANES), F32),
            pltpu.VMEM(mask.shape, jnp.int32),
            pltpu.VMEM(noise_kernel.shape, F32),
            pltpu.VMEM(smooth_kernel.shape, F32),
            pltpu.SemaphoreType.DMA((8,)),
            pltpu.SemaphoreType.DMA((3,)),
        ],
        compiler_params=PARAMS,
        cost_estimate=pl.CostEstimate(flops=6 << 30, transcendentals=0, bytes_accessed=8 << 20),
        name="inner",
    )(count, *(pltpu.with_memory_space_constraint(a, pltpu.HBM) for a in (mask, noise_kernel, smooth_kernel, x)))


def edge(state, low, ends, pick, taps, noise, signal):
    bands = ends.shape[1]
    gram = jax.ShapeDtypeStruct((PACKED, LANES), F32)
    return pl.pallas_call(
        edge_kernel,
        out_shape=(gram, gram),
        in_specs=[SMEM, pl.BlockSpec(memory_space=pl.ANY), VMEM, VMEM, VMEM, VMEM, VMEM],
        out_specs=(VMEM, VMEM),
        scratch_shapes=[
            pltpu.VMEM((272, bands), BF16),
            pltpu.VMEM((2 * PACKED, LANES), F32),
            pltpu.VMEM((4 * (16 + 12 * PITCH), LANES), F32),
            pltpu.VMEM((192, bands), BF16),
            pltpu.VMEM((96, bands), BF16),
            pltpu.SemaphoreType.DMA((1,)),
        ],
        compiler_params=PARAMS,
        name="edge",
    )(state, low, ends, pick, taps, noise, signal)


def scatter_sum(parts, axis):
    n = lax.axis_size(axis)
    me = lax.axis_index(axis)

    def block(k):
        return [lax.dynamic_index_in_dim(x.reshape(n, -1, LANES), k, 0, keepdims=False) for x in parts]

    got = []
    for d in range(1, n):
        got.append(lax.ppermute(sum(block((me + d) % n)), axis, [(i, (i + d) % n) for i in range(n)]))
    return block(me) + got


def gather_rows(x, axis):
    n = lax.axis_size(axis)
    me = lax.axis_index(axis)
    got = [x] + [lax.ppermute(x, axis, [(i, (i + d) % n) for i in range(n)]) for d in range(1, n)]
    if n == 2:
        return jnp.concatenate([jnp.where(me == 0, got[0], got[1]), jnp.where(me == 0, got[1], got[0])])
    stacked = jnp.stack(got)
    return jnp.concatenate([lax.dynamic_index_in_dim(stacked, (me - j) % n, 0, keepdims=False) for j in range(n)])


def exchange(x):
    return lax.ppermute(x, "sub", [(0, 1), (1, 0)])


def total_sum(keep, send):
    parts = [keep, exchange(send)]
    short = [axis for axis in ("wide", "narrow") if lax.axis_size(axis) <= 4]
    long = tuple(axis for axis in ("wide", "narrow") if axis not in short)
    for axis in short:
        parts = scatter_sum(parts, axis)
    x = sum(parts)
    if long:
        x = lax.psum(x, long)
    for axis in reversed(short):
        x = gather_rows(x, axis)
    return x, exchange(x)


def spread(x, row):
    return jnp.broadcast_to(x[row : row + 1, :], (8, LANES))


def three_parts(x):
    high = x.astype(BF16).astype(F32)
    rest = x - high
    mid = rest.astype(BF16).astype(F32)
    return high, mid, rest - mid


def inverse_factor(tiles):
    lane = lax.broadcasted_iota(jnp.int32, (8, LANES), 1)
    sub = lax.broadcasted_iota(jnp.int32, (8, LANES), 0)
    tiles = list(tiles)
    count = len(tiles)
    for first in range(0, count, GROUP):
        last = min(first + GROUP, count)
        ahead = None
        done = []
        for step in range(first, last):
            base = step * 8
            inside = (lane >= base) & (lane < base + 8)

            def columns(x, start):
                return [jnp.broadcast_to(x[:, start + c : start + c + 1], (8, LANES)) for c in range(8)]

            head = tiles[step]
            cols = columns(head, base) if ahead is None else ahead
            head = jnp.where(inside, jnp.where(sub == lane - base, 1.0, 0.0), head)
            pivots = jnp.ones((8, LANES), F32)
            pairs = []
            for r in (0, 2, 4, 6):
                q = r + 1
                a, b, c = spread(cols[r], r), spread(cols[q], r), spread(cols[q], q)
                det = a * c - b * b
                inv = 1.0 / det
                ai, bi, ci = a * inv, b * inv, c * inv
                u, v = cols[r], cols[q]
                below = sub > q
                alpha = jnp.where(below, u * ci - v * bi, 0.0)
                beta = jnp.where(below, v * ai - u * bi, 0.0)
                row_r, row_q = spread(head, r), spread(head, q)
                tops = {}
                for k in range(q + 1, 8):
                    tops[k] = (spread(cols[k], r), spread(cols[k], q))
                    cols[k] = cols[k] - alpha * tops[k][0] - beta * tops[k][1]
                ainv = 1.0 / a
                head = head - (alpha + jnp.where(sub == q, b * ainv, 0.0)) * row_r - beta * row_q
                pivots = jnp.where(sub == r, a, jnp.where(sub == q, det * ainv, pivots))
                pairs.append((r, ai, bi, ci, row_r, row_q, tops))
            scaled = head * lax.rsqrt(pivots)
            own = lane <= base + sub
            tiles[step] = jnp.where(own, scaled, 0.0)
            done.append((scaled, jnp.where(own | (lane >= last * 8), scaled, 0.0)))
            ahead = None
            for m in range(step + 1, last):
                tile = tiles[m]
                cols = columns(tile, base)
                if m == step + 1:
                    ahead = columns(tile, base + 8)
                tile = jnp.where(inside, 0.0, tile)
                for r, ai, bi, ci, row_r, row_q, tops in pairs:
                    u, v = cols[r], cols[r + 1]
                    alpha = u * ci - v * bi
                    beta = v * ai - u * bi
                    tile = tile - alpha * row_r - beta * row_q
                    for k in tops:
                        cols[k] = cols[k] - alpha * tops[k][0] - beta * tops[k][1]
                    if m == step + 1:
                        for c in range(8):
                            ahead[c] = ahead[c] - alpha * spread(u, c) - beta * spread(v, c)
                tiles[m] = tile
        if last < count:
            far = lane >= 8 * last
            keep = far | (lane < 8 * first)
            left = three_parts(jnp.concatenate([jnp.where(far, x, 0.0) for x, _ in done], axis=0))
            right = three_parts(jnp.concatenate([y for _, y in done], axis=0))
            left = jnp.concatenate([left[k] for k in (0, 0, 1, 0, 1, 2)], axis=0).astype(BF16)
            right = jnp.concatenate([right[k] for k in (0, 1, 0, 2, 1, 0)], axis=0).astype(BF16)
            update = lax.dot_general(left, right, (((0,), (0,)), ((), ())), preferred_element_type=F32)
            for m in range(last, count):
                tiles[m] = jnp.where(keep, tiles[m], 0.0) - update[8 * m : 8 * m + 8]
    return tiles


def split_parts(x):
    return [part.astype(BF16) for part in three_parts(x)]


def stacked(a, parts, side=0):
    n = a.shape[0]
    rows = jnp.concatenate(split_parts(a), axis=0)
    first, second, third = [
        lax.dot_general(rows[: (3 - k) * n], part, (((1,), (side,)), ((), ())), preferred_element_type=F32)
        for k, part in enumerate(parts)
    ]
    small = first[2 * n :] + second[n:] + third
    return first[:n] + (first[n : 2 * n] + second[:n] + small)


def factor_block(block):
    tiles = [block[8 * m : 8 * m + 8, :] for m in range(block.shape[0] // 8)]
    return jnp.concatenate(inverse_factor(tiles), axis=0)


def widen(x, width):
    return jnp.concatenate([x, jnp.zeros((x.shape[0], width - x.shape[1]), x.dtype)], axis=1)


def unpack(sums, start):
    r = lax.broadcasted_iota(jnp.int32, (LANES, LANES), 0)
    c = lax.broadcasted_iota(jnp.int32, (LANES, LANES), 1)
    part = lambda first, rows: sums[pl.ds(start + first, rows), :]
    square = part(SQUARE, LANES)
    turned = square.T
    corner = jnp.where(r >= c, square, turned)
    second = jnp.where(r == c, part(LAST + 47, 1), jnp.where(r < c, square, turned))
    blocks = [
        (corner, part(BELOW[0], USED - 128)),
        (second, part(BELOW[1], USED - 256)),
        (part(THIRD, LANES), part(BELOW[2], USED - 384)),
    ]
    return [jnp.concatenate(pair, axis=0) for pair in blocks] + [part(LAST, USED - 384)]


def fill_unit(block):
    r = lax.broadcasted_iota(jnp.int32, block.shape, 0)
    c = lax.broadcasted_iota(jnp.int32, block.shape, 1)
    return jnp.where((r >= VALID - 384) | (c >= VALID - 384), jnp.where(r == c, 1.0, 0.0), block)


def finish_kernel(side_ref, mine_ref, other_ref, pick_ref, start_ref, out_ref, sums, signal, inverse):
    side = side_ref[0]
    sums[pl.ds(pl.multiple_of(side * PACKED, 8), PACKED), :] = mine_ref[...]
    sums[pl.ds(pl.multiple_of((1 - side) * PACKED, 8), PACKED), :] = other_ref[...]

    signal[...] = jnp.zeros_like(signal)
    panels = unpack(sums, PACKED)
    panels[3] = fill_unit(panels[3])
    for panel in range(4):
        low = panel * LANES
        signal[low:USED, low : low + LANES] = panels[panel]
        for other in range(panel + 1, 4):
            first = other * LANES
            size = min(LANES, USED - first)
            signal[low : low + LANES, first : first + size] = panels[panel][first - low : first - low + size].T
    basis = mm(start_ref[...], pick_ref[...].astype(F32), ((0,), (0,)))[:, :USED]

    total = 64.0 * sums[LAST + 46 : LAST + 47, :]
    panels = [block / total for block in unpack(sums, 0)]
    panels[3] = fill_unit(panels[3])
    inverse[...] = jnp.zeros_like(inverse)
    known = None
    for j in range(4):
        low = j * LANES
        size = min(LANES, USED - low)
        own = factor_block(panels[j][:size])
        inverse[low : low + size, low : low + LANES] = own
        if j == 3:
            inverse[low:USED, :low] = -mm(own[:, :size], known)
            break
        below = mm(panels[j][LANES:], own, ((1,), (1,)))
        for k in range(j + 1, 4):
            skip = (k - j - 1) * LANES
            width = min(LANES, USED - k * LANES)
            update = mm(below[skip:], below[skip : skip + width], ((1,), (1,)))
            panels[k] = panels[k] - (update if width == LANES else widen(update, LANES))
        gain = mm(below, own)
        if j == 0:
            known = gain
        else:
            left = -mm(own, known[:LANES])
            inverse[low : low + LANES, :low] = left
            known = jnp.concatenate([known[LANES:] + mm(below, left), gain], axis=1)

    inverse_parts = split_parts(inverse[...])
    signal_parts = split_parts(signal[...])
    turned = stacked(basis, inverse_parts)
    mapped = stacked(stacked(turned[:, :USED], signal_parts), inverse_parts, 1)
    for sweep in range(SWEEPS):
        square = mm(mapped, mapped, ((1,), (1,)))
        turned = stacked(mapped, inverse_parts)
        if sweep + 1 < SWEEPS:
            ahead = stacked(stacked(turned[:, :USED], signal_parts), inverse_parts, 1)
        scale = factor_block(square)
        if sweep + 1 < SWEEPS:
            mapped = mm(scale, ahead)
    weights = mm(scale, turned).astype(BF16)
    out_ref[...] = lax.dot_general(
        pick_ref[...], weights, (((1,), (1,)), ((), ())), preferred_element_type=F32
    ).astype(BF16)


def finish(side, mine, other, pick, start_basis):
    vmem = pl.BlockSpec(memory_space=pltpu.VMEM)
    return pl.pallas_call(
        finish_kernel,
        out_shape=jax.ShapeDtypeStruct((512, LANES), BF16),
        in_specs=[pl.BlockSpec(memory_space=pltpu.SMEM)] + [vmem] * 4,
        out_specs=vmem,
        scratch_shapes=[
            pltpu.VMEM((2 * PACKED, LANES), F32),
            pltpu.VMEM((USED, 512), F32),
            pltpu.VMEM((USED, 512), F32),
        ],
        compiler_params=pltpu.CompilerParams(vmem_limit_bytes=20 << 20),
    )(side, mine, other, pick, start_basis)


def local(radiance, band_mask, row_counts, noise_kernel, smooth_kernel, start_basis):
    height, across, bands = radiance.shape
    count = row_counts[0]
    chain = 1
    for axis in AXES:
        chain *= lax.axis_size(axis)
    up = [(i, i + 1) for i in range(chain - 1)]
    row = jnp.arange(height, dtype=jnp.int32)
    zero = jnp.zeros((), radiance.dtype)
    flat = radiance.reshape(height * across, bands)
    tail = jnp.where((row[-4:] < count)[:, None, None], radiance[-4:], zero).reshape(4 * across, bands)
    tail = jnp.concatenate([tail, jnp.full((16, bands), count, radiance.dtype)], axis=0)
    low = lax.ppermute(tail, AXES, up)

    noise, signal, pick, taps, ends = inner(row_counts, band_mask[None], noise_kernel, smooth_kernel, flat)
    side = lax.axis_index("sub")
    place_in_chain = lax.axis_index(AXES)
    state = jnp.stack([count, side, place_in_chain == 0, place_in_chain == chain - 1, height]).astype(jnp.int32)
    keep, send = edge(state, low, ends, pick, taps, noise, signal)
    mine, other = total_sum(keep, send)
    weights = finish(state[1:2], mine, other, pick, start_basis)
    keep = jnp.repeat(row < count, across)
    masked = jnp.where(keep[:, None], flat, zero)
    result = jnp.dot(masked, weights, preferred_element_type=F32)
    return result.reshape(height, across, weights.shape[1])


def solution(mesh):
    split = P(("groups",) + AXES)
    return jax.shard_map(
        local,
        mesh=mesh,
        in_specs=(P(("groups",) + AXES, None, None), P(), split, P(), P(), P()),
        out_specs=P(("groups",) + AXES, None, None),
        check_vma=False,
    )
```
